128 devices in a mesh: row: 8 (over y, core), col: 16 (over x, z).
Axes of the slice: x: 4, y: 4, z: 4, core: 2. Of those that a mesh axis runs over, the one named last changes fastest.
Arguments:
- contribution: float32 [8, 8, 4, 16, 128, 128], P(None, 'row', None, 'col'), may hold values from -6 to 6
- parent_tiles: float32 [16, 8, 8, 16, 128, 128], P(None, 'row', None, 'col'), may hold values from -6 to 6
- row_basis: float32 [8, 8, 64, 128], P(None, 'row'), may hold values from -2.4 to 2.4
- pivot_basis: float32 [8, 8, 64, 2048], P(None, 'row', None, 'col'), may hold values from -0.125 to 0.125
- tile_ranks: int32 [64], replicated, may hold values from 16 to 64, as said below
- block_map: int32 [64], replicated, may hold values from 0 to 127, as said below
- panel_start: int32 [1], replicated, may hold values from 0 to 63
- pivot_inverse: float32 [512, 512], replicated
Outputs:
- updated_parent: float32 [16, 8, 8, 16, 128, 128], P(None, 'row', None, 'col')
The draws below stay inside these ranges and needn't reach their ends.
Inputs may be any that keep to these rules, and one draw needn't show every extreme that they name: `tile_ranks`: multiples of 16; both 16 and 64 occur. `block_map`: child tile row u * 16 + l, for 0 <= l < 16, maps to parent tile row 2 * 16 * u + h_u + l with 0 <= h_u < 16; the 4 values h_u are distinct modulo 8.
All inputs are finite; a program needn't handle non-finite values.
Results may differ from the reference program's by a relative error of at most 0.0003.
Values sent between devices are 32-bit elements; how exact they have to be, the bound alone decides.
No kernel may reach another device: no remote copies, remote signals or barrier semaphores. Data moves between devices by JAX's collectives and lax.ppermute only.
A program may use at most 128 MiB of HBM per device.

```python
import jax
import jax.numpy as jnp
from jax import lax

B = 128
P_SIZE = 2048
RMAX = 64
PANEL_T = 4
CT_COL = 4
GRID_R = 8
GRID_C = 16
NTC = 64
CT_ROW = 8
PT_ROW = 16
PT_COL = 8
PW = 512


def draw_block_map(key, part):
    key_perm, key_coin = jax.random.split(jax.random.fold_in(key, 11))
    residues = jax.random.permutation(key_perm, GRID_R)[:CT_COL]
    coins = jax.random.randint(key_coin, (CT_COL,), 0, GRID_C // GRID_R)
    shifts = residues + GRID_R * coins
    blocks = jnp.arange(CT_COL)[:, None]
    within = jnp.arange(GRID_C)[None, :]
    return (2 * GRID_C * blocks + shifts[:, None] + within).reshape(-1).astype(jnp.int32)


def draw_tile_ranks(key, part):
    key_rank, key_place = jax.random.split(jax.random.fold_in(key, 23))
    levels = 16 * jax.random.randint(key_rank, (NTC,), 1, RMAX // 16 + 1)
    order = jax.random.permutation(key_place, NTC)
    levels = levels.at[order[0]].set(RMAX).at[order[1]].set(16)
    return levels.astype(jnp.int32)


def draw_pivot_inverse(key, part):
    key_noise = jax.random.fold_in(key, 37)
    noise = jnp.clip(jax.random.normal(key_noise, (PW, PW), jnp.float32), -4.0, 4.0)
    matrix = jnp.eye(PW, dtype=jnp.float32) + 0.5 * noise / jnp.sqrt(jnp.float32(PW))
    return (matrix / (2.0 * jnp.sqrt(jnp.float32(PW)))).astype(jnp.float32)


def shard_levels(rng, dims, cuts, smallest, top_value):
    gain, own = 1.0, jax.random.fold_in(rng, 6)
    for axis_at, blocks in cuts:
        draws = jnp.exp(jax.random.uniform(jax.random.fold_in(own, axis_at), (blocks,), jnp.float32, smallest / len(cuts), top_value / len(cuts)))
        gain = gain * jnp.repeat(draws, dims[axis_at] // blocks).reshape([-1 if axis == axis_at else 1 for axis in range(len(dims))])
    return gain


def normal_values(stream_key, shape, width, bound, cuts=(), held_as=jnp.bfloat16):
    loudness = shard_levels(stream_key, shape, cuts, -0.22, 0.18) if cuts else 1.0
    array = jax.random.normal(stream_key, shape, jnp.float32) * width * loudness
    return jnp.minimum(jnp.maximum(array, -bound), bound).astype(held_as)


def setup_inputs(seed: int = 0) -> dict:
    splits = jax.random.split(jax.random.key(seed), 9)
    return {
        "contribution": normal_values(splits[0], (CT_ROW, GRID_R, CT_COL, GRID_C, B, B), 1.0, 6.0, ((1, 8), (3, 16)), jnp.float32),
        "parent_tiles": normal_values(splits[1], (PT_ROW, GRID_R, PT_COL, GRID_C, B, B), 1.0, 6.0, ((1, 8), (3, 16)), jnp.float32),
        "row_basis": normal_values(splits[2], (CT_ROW, GRID_R, RMAX, B), 0.4, 2.4, ((1, 8),), jnp.float32),
        "pivot_basis": normal_values(splits[3], (CT_ROW, GRID_R, RMAX, P_SIZE), P_SIZE ** -0.5, 0.125, ((1, 8), (3, 16)), jnp.float32),
        "tile_ranks": draw_tile_ranks(jax.random.fold_in(splits[8], 71), 0),
        "block_map": draw_block_map(jax.random.fold_in(splits[8], 71), 0),
        "panel_start": jax.random.randint(splits[6], (1,), 0, NTC).astype(jnp.int32),
        "pivot_inverse": draw_pivot_inverse(jax.random.fold_in(splits[8], 71), 0),
    }


highest = lax.Precision.HIGHEST


def reference(contribution, parent_tiles, row_basis, pivot_basis, tile_ranks, block_map, panel_start, pivot_inverse):
    child_total = contribution.shape[0] * contribution.shape[1]
    parent_total = parent_tiles.shape[0] * parent_tiles.shape[1]
    tile_size = contribution.shape[4]
    rank_max = row_basis.shape[2]
    kept_cols = (jnp.arange(rank_max, dtype=jnp.int32)[None, :] < tile_ranks[:, None]).astype(jnp.float32)
    bases = row_basis.reshape(child_total, rank_max, tile_size) * kept_cols[:, :, None]
    pivots = pivot_basis.reshape(child_total * rank_max, -1)
    gram = jnp.dot(pivots, pivots.T, precision=highest, preferred_element_type=jnp.float32)
    gram = gram.reshape(child_total, rank_max, child_total, rank_max)
    half_product = jnp.einsum("irx,irju->ixju", bases, gram, precision=highest, preferred_element_type=jnp.float32)
    update = jnp.einsum("ixju,juy->ijxy", half_product, bases, precision=highest, preferred_element_type=jnp.float32)
    tile_index = jnp.arange(child_total, dtype=jnp.int32)
    lower_mask = tile_index[:, None] >= tile_index[None, :]
    blocks = contribution.reshape(child_total, child_total, tile_size, tile_size)
    moved_tiles = jnp.where(lower_mask[:, :, None, None], blocks - update, jnp.float32(0.0))
    parent_grid = parent_tiles.reshape(parent_total, parent_total, tile_size, tile_size)
    assembled = parent_grid.at[block_map[:, None], block_map[None, :]].add(moved_tiles)
    start_col = panel_start[0].astype(jnp.int32)
    panel = lax.dynamic_slice_in_dim(assembled, start_col, PANEL_T, axis=1)
    row_panel = jnp.transpose(panel, (0, 2, 1, 3)).reshape(parent_total, tile_size, PANEL_T * tile_size)
    scaled = jnp.einsum("axp,pq->axq", row_panel, pivot_inverse, precision=highest, preferred_element_type=jnp.float32)
    col_index = jnp.arange(parent_total, dtype=jnp.int32)

    def trailing_row(inputs):
        row_id, current, scaled_row = inputs
        trailing = jnp.einsum("xq,byq->bxy", scaled_row, row_panel, precision=highest, preferred_element_type=jnp.float32)
        window = (row_id >= col_index) & (col_index >= start_col + PANEL_T)
        return jnp.where(window[:, None, None], current - trailing, current)

    result = lax.map(trailing_row, (col_index, assembled, scaled))
    return result.reshape(parent_tiles.shape)
```

```python
import jax
import jax.numpy as jnp
from jax import lax
from jax.experimental import pallas as pl
from jax.experimental.pallas import tpu as pltpu
from jax.sharding import PartitionSpec as P

PANEL_T = 4
F32 = jnp.float32
BF16 = jnp.bfloat16


def shift_of(meta, u):
    return meta[16 * u] - 32 * u


def chunk_of(meta, rho):
    row = meta[129]
    side = (rho + row) & 1
    return 4 * side + (((row >> 1) - (rho >> 1)) & 3)


def row_source(meta, u):
    return (meta[129] - shift_of(meta, u)) & 7


def col_source(meta, s, col):
    return (col - shift_of(meta, s)) & 15


def split2(x):
    hi = x.astype(BF16)
    return hi, (x - hi.astype(F32)).astype(BF16)


def dot3(a, b, dims):
    dn = (dims, ((), ()))
    ah, al = a
    bh, bl = b
    low = lax.dot_general(ah, bl, dn, preferred_element_type=F32)
    low += lax.dot_general(al, bh, dn, preferred_element_type=F32)
    return lax.dot_general(ah, bh, dn, preferred_element_type=F32) + low


NT = ((1,), (1,))
NN = ((1,), (0,))
TN = ((0,), (0,))


def row_perm(x, dy, dc):
    pairs = [(2 * y + k, 2 * ((y + dy) % 4) + (k + dc) % 2) for y in range(4) for k in range(2)]
    return lax.ppermute(x, "row", pairs)


def col_perm(x, dx, dz):
    pairs = [(4 * a + b, 4 * ((a + dx) % 4) + (b + dz) % 4) for a in range(4) for b in range(4)]
    return lax.ppermute(x, "col", pairs)


def gather_rows(x):
    ring = jnp.stack([x] + [row_perm(x, d, 0) for d in (1, 2, 3)])
    return jnp.concatenate([ring, row_perm(ring, 0, 1)])


def rotate(x, axis, count, by):
    def step(k):
        pairs = [(i, (i + k) % count) for i in range(count)]
        return (lambda v: lax.ppermute(v, axis, pairs)) if k else (lambda v: v)

    return lax.switch(by, [step(k) for k in range(count)], x)


def products_kernel(meta, v_ref, *refs):
    a_refs, b_refs = refs[0:4], refs[4:8]
    hi_ref, lo_ref = refs[8], refs[9]
    for u in range(4):
        own = v_ref[chunk_of(meta, row_source(meta, u)), 2 * u : 2 * u + 2]
        hi, lo = split2(own.reshape(128, 128))
        hi_ref[128 * u : 128 * u + 128] = hi
        lo_ref[128 * u : 128 * u + 128] = lo

    def left(first, last):
        return hi_ref[first:last], lo_ref[first:last]

    def right(col, s, q):
        parts = []
        for k in (s, q):
            j = col_source(meta, k, col)
            parts.append(v_ref[chunk_of(meta, j & 7), 2 * k + (j >> 3)])
        return split2(jnp.concatenate(parts, axis=0))

    col = meta[130]
    x, z = col >> 2, col & 3
    low_half = lax.broadcasted_iota(jnp.int32, (128, 128), 1) < 64
    for d in range(4):

        def upper(e, carry):
            other = 4 * ((x + e) & 3) + ((z + d) & 3)
            a_refs[d][e] = dot3(left(128, 448), right(other, 0, 1), NT)
            return carry

        def lower(e, carry):
            other = 4 * ((x + d) & 3) + ((z + e) & 3)
            b_refs[d][e, 0:64] = dot3(left(448, 512), right(other, 0, 1), NT)
            ends = right(other, 0, 3)
            b_refs[d][e, 64:192] = jnp.where(
                low_half, dot3(left(0, 128), ends, NT), dot3(left(384, 512), ends, NT)
            )
            mid = right(other, 2, 2)
            b_refs[d][e, 192:320] = jnp.where(
                low_half, dot3(left(256, 384), mid, NT), dot3(left(384, 512), mid, NT)
            )
            return carry

        lax.fori_loop(0, 4, upper, 0)
        lax.fori_loop(0, 4, lower, 0)


def products(meta, pivots):
    whole = pl.BlockSpec(memory_space=pltpu.VMEM)
    return pl.pallas_call(
        products_kernel,
        grid_spec=pltpu.PrefetchScalarGridSpec(
            num_scalar_prefetch=1,
            grid=(),
            in_specs=[whole],
            out_specs=[whole] * 8,
            scratch_shapes=[pltpu.VMEM((512, 128), BF16)] * 2,
        ),
        out_shape=[jax.ShapeDtypeStruct((4, 320, 128), F32)] * 8,
        compiler_params=pltpu.CompilerParams(vmem_limit_bytes=24 << 20),
        cost_estimate=pl.CostEstimate(flops=2 * 10**9, bytes_accessed=8 << 20, transcendentals=0),
    )(meta, pivots)


def scatter_sums(parts, first, second):
    arrived = [parts[0]] + [first(parts[d], d) for d in (1, 2, 3)]
    sums = [arrived[0][e] + arrived[1][e] + arrived[2][e] + arrived[3][e] for e in range(4)]
    return [sums[0]] + [second(sums[e], e) for e in (1, 2, 3)]


def moved_kernel(meta, *refs):
    wa, wb = refs[0:4], refs[4:8]
    base_ref, c_refs, parent_ref = refs[8], refs[9:13], refs[13]
    out_ref, pcol_ref = refs[14], refs[15]
    g_ref = refs[16]
    col = meta[130]
    rank_rows = lax.broadcasted_iota(jnp.int32, (64, 128), 0)

    def basis(rho, t, tile):
        return jnp.where(rank_rows < meta[64 + tile], base_ref[chunk_of(meta, rho), t], 0.0)

    def col_basis(s):
        j = col_source(meta, s, col)
        return basis(j & 7, 2 * s + (j >> 3), 16 * s + j)

    bj = [col_basis(s) for s in range(4)]
    zero = jnp.zeros((64, 128), F32)

    def diagonal(s, q):
        top = jnp.concatenate([bj[s], zero], axis=1)
        bottom = jnp.concatenate([zero, bj[q]], axis=1)
        return split2(jnp.concatenate([top, bottom], axis=0))

    d01, d03, d22 = diagonal(0, 1), diagonal(0, 3), diagonal(2, 2)
    a_sum = wa[0][...] + wa[1][...] + wa[2][...] + wa[3][...]
    b_sum = wb[0][...] + wb[1][...] + wb[2][...] + wb[3][...]
    g_ref[0:320] = dot3(split2(a_sum), d01, NN)
    g_ref[320:384] = dot3(split2(b_sum[0:64]), d01, NN)
    g_ref[384:512] = dot3(split2(b_sum[64:192]), d03, NN)
    g_ref[512:640] = dot3(split2(b_sum[192:320]), d22, NN)

    for t in range(8):
        u, w = t // 2, t % 2
        rho = row_source(meta, u)
        bi = split2(basis(rho, t, 16 * u + 8 * w + rho))

        def put(s, tile):
            value = c_refs[s][2 * (u - s) + w] - tile
            if u == s:
                keep = rho + 8 * w >= col_source(meta, s, col)
                value = jnp.where(keep, value, 0.0)
            out_ref[u * (u + 1) + w * (u + 1) + s] = value

        def update(first, lane, wide):
            return dot3(bi, split2(g_ref[first : first + 64, lane : lane + wide]), TN)

        if t >= 2:
            both = update(64 * (t - 2), 0, 256)
            put(0, both[:, 0:128])
            put(1, both[:, 128:256])
        else:
            put(0, update(384 + 64 * t, 0, 128))
        if u == 2:
            put(2, update(512 + 64 * w, 0, 128))
        if u == 3:
            put(2, update(512 + 64 * w, 128, 128))
            put(3, update(384 + 64 * w, 128, 128))

    start = meta[128]
    place = (col - start) & 15
    tile_col = start + place
    b = tile_col >> 4
    s = b >> 1

    def add(a, carry):
        u = a >> 2
        tile_row = 8 * a + meta[129]
        at = tile_row - meta[16 * u]
        at_col = tile_col - meta[16 * s]
        use = (at >= 0) & (at < 16) & (at_col >= 0) & (at_col < 16) & (u >= s)
        index = jnp.where(use, u * (u + 1) + (at >> 3) * (u + 1) + s, 0)
        pcol_ref[a] = parent_ref[a, 0, 0, 0] + jnp.where(use, out_ref[index], 0.0)
        return carry

    lax.fori_loop(0, 16, add, 0)


def panel_block(meta):
    start = meta[128]
    return jnp.minimum((start + ((meta[130] - start) & 15)) >> 4, 7)


def moved_tiles(meta, wa, wb, bases, cols, parent_tiles):
    whole = pl.BlockSpec(memory_space=pltpu.VMEM)
    parent_spec = pl.BlockSpec(
        (16, 1, 1, 1, 128, 128), lambda i, meta: (0, 0, panel_block(meta), 0, 0, 0)
    )
    return pl.pallas_call(
        moved_kernel,
        grid_spec=pltpu.PrefetchScalarGridSpec(
            num_scalar_prefetch=1,
            grid=(1,),
            in_specs=[whole] * 13 + [parent_spec],
            out_specs=[whole, whole],
            scratch_shapes=[pltpu.VMEM((640, 256), F32)],
        ),
        out_shape=[
            jax.ShapeDtypeStruct((20, 128, 128), F32),
            jax.ShapeDtypeStruct((16, 128, 128), F32),
        ],
        compiler_params=pltpu.CompilerParams(vmem_limit_bytes=32 << 20),
        cost_estimate=pl.CostEstimate(flops=10**9, bytes_accessed=8 << 20, transcendentals=0),
    )(meta, *wa, *wb, bases, *cols, parent_tiles)


def scaled_kernel(meta, got_ref, inverse_ref, panel_ref, sa_ref, sb_ref):
    start = meta[128]
    tiles = [got_ref[(start + p) & 15] for p in range(PANEL_T)]
    panel = jnp.concatenate(tiles, axis=1)
    panel_ref[...] = panel
    out = dot3(split2(panel), split2(inverse_ref[...]), NN)
    sa_ref[...] = out[0:64]
    sb_ref[...] = out[64:128]


def scale_panel(meta, got, inverse):
    whole = pl.BlockSpec(memory_space=pltpu.VMEM)
    return pl.pallas_call(
        scaled_kernel,
        grid_spec=pltpu.PrefetchScalarGridSpec(
            num_scalar_prefetch=1, grid=(), in_specs=[whole] * 2, out_specs=[whole] * 3
        ),
        out_shape=[
            jax.ShapeDtypeStruct((128, 512), F32),
            jax.ShapeDtypeStruct((64, 512), F32),
            jax.ShapeDtypeStruct((64, 512), F32),
        ],
        compiler_params=pltpu.CompilerParams(vmem_limit_bytes=24 << 20),
        cost_estimate=pl.CostEstimate(flops=2 * 10**8, bytes_accessed=3 << 20, transcendentals=0),
    )(meta, got, inverse)


def trailing_kernel(
    meta, parent_ref, moved_ref, sa_ref, sb_ref, panel_ref, out_ref, sh_ref, sl_ref, ph_ref, pl_ref
):
    q, g = pl.program_id(0), pl.program_id(1)
    row, col, start = meta[129], meta[130], meta[128]
    x, z = col >> 2, col & 3

    @pl.when(q == 0)
    def _():
        for k in range(4):
            a = 4 * g + k
            e, d = (x - (a >> 2)) & 3, (z - (a & 3)) & 3
            hi, lo = split2(sa_ref[4 * e + d])
            sh_ref[g, 128 * k : 128 * k + 64] = hi
            sl_ref[g, 128 * k : 128 * k + 64] = lo
            hi, lo = split2(sb_ref[4 * d + e])
            sh_ref[g, 128 * k + 64 : 128 * k + 128] = hi
            sl_ref[g, 128 * k + 64 : 128 * k + 128] = lo

    @pl.when(g == 0)
    def _():
        for k in range(2):
            hi, lo = split2(panel_ref[chunk_of(meta, 2 * q + k)])
            ph_ref[128 * k : 128 * k + 128] = hi
            pl_ref[128 * k : 128 * k + 128] = lo

    def assembled(k, j):
        tile_row = 8 * (4 * g + k) + row
        tile_col = 16 * (2 * q + j) + col
        at = tile_row - meta[16 * g]
        at_col = tile_col - meta[16 * q]
        use = (at >= 0) & (at < 16) & (at_col >= 0) & (at_col < 16) & (g >= q)
        index = jnp.where(use, g * (g + 1) + (at >> 3) * (g + 1) + q, 0)
        tile = parent_ref[k, 0, j, 0] + jnp.where(use, moved_ref[index], 0.0)
        return tile, (tile_row >= tile_col) & (tile_col >= start + PANEL_T)

    first_col = 32 * q + col
    active = (32 * g + 24 + row >= first_col) & (first_col + 16 >= start + PANEL_T)

    @pl.when(active)
    def _():
        trailing = dot3((sh_ref[g], sl_ref[g]), (ph_ref[...], pl_ref[...]), NT)
        for k in range(4):
            for j in range(2):
                tile, window = assembled(k, j)
                part = trailing[128 * k : 128 * k + 128, 128 * j : 128 * j + 128]
                out_ref[k, 0, j, 0] = tile - jnp.where(window, part, 0.0)

    @pl.when(jnp.logical_not(active))
    def _():
        for k in range(4):
            for j in range(2):
                out_ref[k, 0, j, 0] = assembled(k, j)[0]


def trailing_update(meta, parent_tiles, moved, sa, sb, panel):
    whole = pl.BlockSpec(memory_space=pltpu.VMEM)
    tiles = pl.BlockSpec((4, 1, 2, 1, 128, 128), lambda q, g, meta: (g, 0, q, 0, 0, 0))
    return pl.pallas_call(
        trailing_kernel,
        grid_spec=pltpu.PrefetchScalarGridSpec(
            num_scalar_prefetch=1,
            grid=(4, 4),
            in_specs=[tiles, whole, whole, whole, whole],
            out_specs=tiles,
            scratch_shapes=[
                pltpu.VMEM((4, 512, 512), BF16),
                pltpu.VMEM((4, 512, 512), BF16),
                pltpu.VMEM((256, 512), BF16),
                pltpu.VMEM((256, 512), BF16),
            ],
        ),
        out_shape=jax.ShapeDtypeStruct(parent_tiles.shape, F32),
        compiler_params=pltpu.CompilerParams(vmem_limit_bytes=40 << 20),
        cost_estimate=pl.CostEstimate(flops=7 * 10**9, bytes_accessed=24 << 20, transcendentals=0),
    )(meta, parent_tiles, moved, sa, sb, panel)


def per_device(
    contribution,
    parent_tiles,
    row_basis,
    pivot_basis,
    tile_ranks,
    block_map,
    panel_start,
    pivot_inverse,
):
    my_row = lax.axis_index("row")
    my_col = lax.axis_index("col")
    meta = jnp.concatenate(
        [block_map, tile_ranks, panel_start, jnp.stack([my_row, my_col])]
    ).astype(jnp.int32)
    shifts = [block_map[16 * u] - 32 * u for u in range(4)]

    pivots = gather_rows(pivot_basis[:, 0])
    by_row = [
        rotate(contribution[2 * u : 2 * u + 2, 0, 0 : u + 1, 0], "row", 8, shifts[u] & 7)
        for u in (3, 2, 1, 0)
    ][::-1]
    bases = gather_rows(row_basis[:, 0])
    parts = products(meta, pivots)
    wa = scatter_sums(parts[0:4], lambda v, d: col_perm(v, 0, d), lambda v, d: col_perm(v, d, 0))
    wb = scatter_sums(parts[4:8], lambda v, d: col_perm(v, d, 0), lambda v, d: col_perm(v, 0, d))
    cols = [
        rotate(
            jnp.concatenate([by_row[u][:, s] for u in range(s, 4)]), "col", 16, shifts[s]
        )
        for s in range(4)
    ]
    moved, panel_col = moved_tiles(meta, wa, wb, bases, cols, parent_tiles)
    got = lax.all_to_all(panel_col, "col", split_axis=0, concat_axis=0, tiled=True)
    panel, sa, sb = scale_panel(meta, got, pivot_inverse)

    turn = []
    for r in range(8):
        for c in range(16):
            turn.append((16 * r + c, 16 * (c // 2) + 8 * (c % 2) + r))
    panel = gather_rows(lax.ppermute(panel, ("row", "col"), turn))
    ring_a = jnp.stack([sa] + [col_perm(sa, 0, d) for d in (1, 2, 3)])
    ring_b = jnp.stack([sb] + [col_perm(sb, d, 0) for d in (1, 2, 3)])
    sa = jnp.concatenate([ring_a] + [col_perm(ring_a, d, 0) for d in (1, 2, 3)])
    sb = jnp.concatenate([ring_b] + [col_perm(ring_b, 0, d) for d in (1, 2, 3)])
    return trailing_update(meta, parent_tiles, moved, sa, sb, panel)


def solution(mesh):
    placed = (
        P(None, "row", None, "col", None, None),
        P(None, "row", None, "col", None, None),
        P(None, "row", None, None),
        P(None, "row", None, "col"),
        P(),
        P(),
        P(),
        P(),
    )
    return jax.shard_map(
        per_device,
        mesh=mesh,
        in_specs=placed,
        out_specs=P(None, "row", None, "col", None, None),
        check_vma=False,
    )
```

```python
import jax
import jax.numpy as jnp
from jax import lax
from jax.experimental import pallas as pl
from jax.experimental.pallas import tpu as pltpu
from jax.sharding import PartitionSpec as P

PANEL_T = 4
F32 = jnp.float32
BF16 = jnp.bfloat16


def shift_of(meta, u):
    return meta[16 * u] - 32 * u


def gathered_row(meta, k):
    row = meta[129]
    return 2 * (((row >> 1) - k % 4) & 3) + ((row + k // 4) & 1)


def row_source(meta, u):
    return (meta[129] - shift_of(meta, u)) & 7


def col_source(meta, s, col):
    return (col - shift_of(meta, s)) & 15


def panel_child(meta, p):
    tile = meta[128] + p
    s = tile >> 5
    at = tile - meta[16 * s]
    return s, at & 15, (at >= 0) & (at < 16)


def split2(x):
    hi = x.astype(BF16)
    return hi, (x - hi.astype(F32)).astype(BF16)


def dot3(a, b, dims):
    dn = (dims, ((), ()))
    ah, al = a
    bh, bl = b
    low = lax.dot_general(ah, bl, dn, preferred_element_type=F32)
    low += lax.dot_general(al, bh, dn, preferred_element_type=F32)
    return lax.dot_general(ah, bh, dn, preferred_element_type=F32) + low


NT = ((1,), (1,))
NN = ((1,), (0,))
TN = ((0,), (0,))


def after(x, *others):
    return lax.optimization_barrier((x,) + others)[0]


def row_perm(x, dy, dc):
    pairs = [(2 * y + k, 2 * ((y + dy) % 4) + (k + dc) % 2) for y in range(4) for k in range(2)]
    return lax.ppermute(x, "row", pairs)


def col_perm(x, dx, dz):
    pairs = [(4 * a + b, 4 * ((a + dx) % 4) + (b + dz) % 4) for a in range(4) for b in range(4)]
    return lax.ppermute(x, "col", pairs)


def gather_rows(x):
    ring = [x] + [row_perm(x, d, 0) for d in (1, 2, 3)]
    return ring + [row_perm(v, 0, 1) for v in ring]


def rotate(x, axis, count, by):
    def step(k):
        pairs = [(i, (i + k) % count) for i in range(count)]
        return (lambda v: lax.ppermute(v, axis, pairs)) if k else (lambda v: v)

    return lax.switch(by, [step(k) for k in range(count)], x)


def across_col(x):
    return lax.all_to_all(x, "col", split_axis=0, concat_axis=0, tiled=True)


def whole():
    return pl.BlockSpec(memory_space=pltpu.VMEM)


def products_kernel(meta, *refs):
    v_refs, a_refs, b_refs = refs[0:8], refs[8:12], refs[12:16]
    vh_ref, vl_ref, hi_ref, lo_ref = refs[16:20]
    e = pl.program_id(0)

    @pl.when(e == 0)
    def _():
        for k in range(8):
            rho = gathered_row(meta, k)
            hi, lo = split2(v_refs[k][...])
            vh_ref[rho] = hi
            vl_ref[rho] = lo
        for u in range(4):
            rho = row_source(meta, u)
            for w in range(2):
                at = 128 * u + 64 * w
                hi_ref[at : at + 64] = vh_ref[rho, 2 * u + w]
                lo_ref[at : at + 64] = vl_ref[rho, 2 * u + w]

    def left(first, last):
        return hi_ref[first:last], lo_ref[first:last]

    def right(col, s, q):
        places = []
        for k in (s, q):
            j = col_source(meta, k, col)
            places.append((j & 7, 2 * k + (j >> 3)))
        return tuple(
            jnp.concatenate([ref[places[0]], ref[places[1]]], axis=0) for ref in (vh_ref, vl_ref)
        )

    col = meta[130]
    x, z = col >> 2, col & 3
    low_half = lax.broadcasted_iota(jnp.int32, (128, 128), 1) < 64
    for d in range(4):
        other = 4 * ((x + e) & 3) + ((z + d) & 3)
        a_refs[d][0] = dot3(left(128, 448), right(other, 0, 1), NT)
        other = 4 * ((x + d) & 3) + ((z + e) & 3)
        b_refs[d][0, 0:64] = dot3(left(448, 512), right(other, 0, 1), NT)
        ends = right(other, 0, 3)
        b_refs[d][0, 64:192] = jnp.where(
            low_half, dot3(left(0, 128), ends, NT), dot3(left(384, 512), ends, NT)
        )
        mid = right(other, 2, 2)
        b_refs[d][0, 192:320] = jnp.where(
            low_half, dot3(left(256, 384), mid, NT), dot3(left(384, 512), mid, NT)
        )


def products(meta, pivots):
    return pl.pallas_call(
        products_kernel,
        grid_spec=pltpu.PrefetchScalarGridSpec(
            num_scalar_prefetch=1,
            grid=(4,),
            in_specs=[whole()] * 8,
            out_specs=[pl.BlockSpec((1, 320, 128), lambda e, meta: (e, 0, 0))] * 8,
            scratch_shapes=[pltpu.VMEM((8, 8, 64, 128), BF16)] * 2
            + [pltpu.VMEM((512, 128), BF16)] * 2,
        ),
        out_shape=[jax.ShapeDtypeStruct((4, 320, 128), F32)] * 8,
        compiler_params=pltpu.CompilerParams(vmem_limit_bytes=24 << 20),
        cost_estimate=pl.CostEstimate(flops=2 * 10**9, bytes_accessed=8 << 20, transcendentals=0),
    )(meta, *pivots)


def scatter_sums(parts, first, second):
    arrived = [parts[0]] + [first(parts[d], d) for d in (1, 2, 3)]
    sums = [arrived[0][e] + arrived[1][e] + arrived[2][e] + arrived[3][e] for e in range(4)]
    return [sums[0]] + [second(sums[e], e) for e in (1, 2, 3)]


def send_kernel(meta, *refs):
    v_refs, c_refs, out_ref, v_ref = refs[0:8], refs[8:12], refs[12], refs[13]
    for k in range(8):
        v_ref[gathered_row(meta, k)] = v_refs[k][...]
    own = jnp.concatenate(
        [v_ref[row_source(meta, u), 2 * u + w] for u in range(4) for w in range(2)], axis=0
    )
    own = split2(own)

    def pair(p):
        parts = []
        for k in (p, p + 1):
            s, at, _ = panel_child(meta, k)
            parts.append(v_ref[at & 7, 2 * s + (at >> 3)])
        return split2(jnp.concatenate(parts, axis=0))

    first, second = dot3(own, pair(0), NT), dot3(own, pair(2), NT)
    start, col = meta[128], meta[130]
    mine = jnp.int32(0)
    for s in range(1, 4):
        p = meta[16 * s] + col - start
        mine = jnp.where((p >= 0) & (p < PANEL_T), s, mine)
    for u in range(4):
        rho = row_source(meta, u)
        for w in range(2):
            t = 2 * u + w
            slot = (meta[16 * u] + 8 * w + rho) >> 3
            out_ref[slot, 1, 0:64] = first[64 * t : 64 * t + 64]
            out_ref[slot, 1, 64:128] = second[64 * t : 64 * t + 64]
            out_ref[slot, 0] = c_refs[u][w, jnp.minimum(mine, u)]


def panel_send(meta, pivots, by_row):
    return pl.pallas_call(
        send_kernel,
        grid_spec=pltpu.PrefetchScalarGridSpec(
            num_scalar_prefetch=1,
            grid=(),
            in_specs=[whole()] * 12,
            out_specs=whole(),
            scratch_shapes=[pltpu.VMEM((8, 8, 64, 128), F32)],
        ),
        out_shape=jax.ShapeDtypeStruct((16, 2, 128, 128), F32),
        compiler_params=pltpu.CompilerParams(vmem_limit_bytes=24 << 20),
        cost_estimate=pl.CostEstimate(flops=5 * 10**8, bytes_accessed=5 << 20, transcendentals=0),
    )(meta, *pivots, *by_row)


def masked_basis(meta, ref, rho, t, tile):
    rows = lax.broadcasted_iota(jnp.int32, (64, 128), 0)
    return jnp.where(rows < meta[64 + tile], ref[rho, t], 0.0)


def block_diagonal(first, second):
    zero = jnp.zeros((64, 128), F32)
    top = jnp.concatenate([first, zero], axis=1)
    bottom = jnp.concatenate([zero, second], axis=1)
    return split2(jnp.concatenate([top, bottom], axis=0))


def panel_kernel(meta, *refs):
    base_refs, parent_ref, got_ref, inverse_ref = refs[0:8], refs[8], refs[9], refs[10]
    panel_ref, sa_ref, sb_ref, base_ref = refs[11:15]
    for k in range(8):
        base_ref[gathered_row(meta, k)] = base_refs[k][...]
    row, col, start = meta[129], meta[130], meta[128]
    u = col >> 2
    at = 8 * col + row - meta[16 * u]
    row_ok = (at >= 0) & (at < 16)
    at = at & 15
    tile = 16 * u + at
    bi = split2(masked_basis(meta, base_ref, at & 7, 2 * u + (at >> 3), tile))
    weights = got_ref[0, 1]
    for k in range(1, 16):
        weights = weights + got_ref[k, 1]
    bj, keep, place = [], [], []
    for p in range(PANEL_T):
        s, at_col, col_ok = panel_child(meta, p)
        other = 16 * s + at_col
        bj.append(masked_basis(meta, base_ref, at_col & 7, 2 * s + (at_col >> 3), other))
        keep.append(row_ok & col_ok & (tile >= other))
        place.append(at_col)
    half = [
        dot3(split2(weights[0:64]), block_diagonal(bj[0], bj[1]), NN),
        dot3(split2(weights[64:128]), block_diagonal(bj[2], bj[3]), NN),
    ]
    update = dot3(bi, split2(jnp.concatenate(half, axis=1)), TN)
    tiles = []
    for p in range(PANEL_T):
        moved = got_ref[place[p], 0] - update[:, 128 * p : 128 * p + 128]
        tiles.append(parent_ref[(start + p) & 15] + jnp.where(keep[p], moved, 0.0))
    panel = jnp.concatenate(tiles, axis=1)
    panel_ref[...] = panel
    out = dot3(split2(panel), split2(inverse_ref[...]), NN)
    sa_ref[...] = out[0:64]
    sb_ref[...] = out[64:128]


def panel_row(meta, bases, parent_panel, got, inverse):
    return pl.pallas_call(
        panel_kernel,
        grid_spec=pltpu.PrefetchScalarGridSpec(
            num_scalar_prefetch=1,
            grid=(),
            in_specs=[whole()] * 11,
            out_specs=[whole()] * 3,
            scratch_shapes=[pltpu.VMEM((8, 8, 64, 128), F32)],
        ),
        out_shape=[
            jax.ShapeDtypeStruct((128, 512), F32),
            jax.ShapeDtypeStruct((64, 512), F32),
            jax.ShapeDtypeStruct((64, 512), F32),
        ],
        compiler_params=pltpu.CompilerParams(vmem_limit_bytes=32 << 20),
        cost_estimate=pl.CostEstimate(flops=4 * 10**8, bytes_accessed=6 << 20, transcendentals=0),
    )(meta, *bases, parent_panel, got, inverse)


def moved_kernel(meta, *refs):
    wa, wb, base_refs, c_refs = refs[0:4], refs[4:8], refs[8:16], refs[16:20]
    out_ref, g_ref, base_ref = refs[20:23]
    for k in range(8):
        base_ref[gathered_row(meta, k)] = base_refs[k][...]
    col = meta[130]
    bj = []
    for s in range(4):
        j = col_source(meta, s, col)
        bj.append(masked_basis(meta, base_ref, j & 7, 2 * s + (j >> 3), 16 * s + j))
    d01, d03, d22 = (block_diagonal(bj[s], bj[q]) for s, q in ((0, 1), (0, 3), (2, 2)))
    a_sum = wa[0][...] + wa[1][...] + wa[2][...] + wa[3][...]
    b_sum = wb[0][...] + wb[1][...] + wb[2][...] + wb[3][...]
    g_ref[0:320] = dot3(split2(a_sum), d01, NN)
    g_ref[320:384] = dot3(split2(b_sum[0:64]), d01, NN)
    g_ref[384:512] = dot3(split2(b_sum[64:192]), d03, NN)
    g_ref[512:640] = dot3(split2(b_sum[192:320]), d22, NN)

    for t in range(8):
        u, w = t // 2, t % 2
        rho = row_source(meta, u)
        bi = split2(masked_basis(meta, base_ref, rho, t, 16 * u + 8 * w + rho))

        def put(s, tile):
            value = c_refs[s][2 * (u - s) + w] - tile
            if u == s:
                keep = rho + 8 * w >= col_source(meta, s, col)
                value = jnp.where(keep, value, 0.0)
            out_ref[u * (u + 1) + w * (u + 1) + s] = value

        def update(first, lane, wide):
            return dot3(bi, split2(g_ref[first : first + 64, lane : lane + wide]), TN)

        if t >= 2:
            both = update(64 * (t - 2), 0, 256)
            put(0, both[:, 0:128])
            put(1, both[:, 128:256])
        else:
            put(0, update(384 + 64 * t, 0, 128))
        if u == 2:
            put(2, update(512 + 64 * w, 0, 128))
        if u == 3:
            put(2, update(512 + 64 * w, 128, 128))
            put(3, update(384 + 64 * w, 128, 128))


def moved_tiles(meta, wa, wb, bases, cols):
    return pl.pallas_call(
        moved_kernel,
        grid_spec=pltpu.PrefetchScalarGridSpec(
            num_scalar_prefetch=1,
            grid=(),
            in_specs=[whole()] * 20,
            out_specs=whole(),
            scratch_shapes=[pltpu.VMEM((640, 256), F32), pltpu.VMEM((8, 8, 64, 128), F32)],
        ),
        out_shape=jax.ShapeDtypeStruct((20, 128, 128), F32),
        compiler_params=pltpu.CompilerParams(vmem_limit_bytes=32 << 20),
        cost_estimate=pl.CostEstimate(flops=10**9, bytes_accessed=6 << 20, transcendentals=0),
    )(meta, *wa, *wb, *bases, *cols)


def trailing_kernel(meta, parent_ref, moved_ref, *refs):
    a_refs, b_refs, panel_refs, out_ref = refs[0:4], refs[4:8], refs[8:16], refs[16]
    sh_ref, sl_ref, ph_ref, pl_ref = refs[17:21]
    q, g = pl.program_id(0), pl.program_id(1)
    row, col, start = meta[129], meta[130], meta[128]
    x, z = col >> 2, col & 3

    @pl.when((q == 0) & (g == 0))
    def _():
        for k in range(8):
            tile = gathered_row(meta, k)
            hi, lo = split2(panel_refs[k][...])
            ph_ref[tile >> 1, tile & 1] = hi
            pl_ref[tile >> 1, tile & 1] = lo
        for m in range(4):
            for n in range(4):
                to = ((x - m) & 3, (z - n) & 3)
                hi, lo = split2(a_refs[m][n])
                sh_ref[to[0], to[1], 0:64] = hi
                sl_ref[to[0], to[1], 0:64] = lo
                to = ((x - n) & 3, (z - m) & 3)
                hi, lo = split2(b_refs[m][n])
                sh_ref[to[0], to[1], 64:128] = hi
                sl_ref[to[0], to[1], 64:128] = lo

    def assembled(k, j):
        tile_row = 8 * (4 * g + k) + row
        tile_col = 16 * (2 * q + j) + col
        at = tile_row - meta[16 * g]
        at_col = tile_col - meta[16 * q]
        use = (at >= 0) & (at < 16) & (at_col >= 0) & (at_col < 16) & (g >= q)
        index = jnp.where(use, g * (g + 1) + (at >> 3) * (g + 1) + q, 0)
        tile = parent_ref[k, 0, j, 0] + jnp.where(use, moved_ref[index], 0.0)
        return tile, (tile_row >= tile_col) & (tile_col >= start + PANEL_T)

    first_col = 32 * q + col
    active = (32 * g + 24 + row >= first_col) & (first_col + 16 >= start + PANEL_T)

    @pl.when(active)
    def _():
        left = (sh_ref[g].reshape(512, 512), sl_ref[g].reshape(512, 512))
        right = (ph_ref[q].reshape(256, 512), pl_ref[q].reshape(256, 512))
        trailing = dot3(left, right, NT)
        for k in range(4):
            for j in range(2):
                tile, window = assembled(k, j)
                part = trailing[128 * k : 128 * k + 128, 128 * j : 128 * j + 128]
                out_ref[k, 0, j, 0] = tile - jnp.where(window, part, 0.0)

    @pl.when(jnp.logical_not(active))
    def _():
        for k in range(4):
            for j in range(2):
                out_ref[k, 0, j, 0] = assembled(k, j)[0]


def trailing_update(meta, parent_tiles, moved, sa, sb, panel):
    tiles = pl.BlockSpec((4, 1, 2, 1, 128, 128), lambda q, g, meta: (g, 0, q, 0, 0, 0))
    return pl.pallas_call(
        trailing_kernel,
        grid_spec=pltpu.PrefetchScalarGridSpec(
            num_scalar_prefetch=1,
            grid=(4, 4),
            in_specs=[tiles] + [whole()] * 17,
            out_specs=tiles,
            scratch_shapes=[pltpu.VMEM((4, 4, 128, 512), BF16)] * 2
            + [pltpu.VMEM((4, 2, 128, 512), BF16)] * 2,
        ),
        out_shape=jax.ShapeDtypeStruct(parent_tiles.shape, F32),
        compiler_params=pltpu.CompilerParams(vmem_limit_bytes=40 << 20),
        cost_estimate=pl.CostEstimate(flops=7 * 10**9, bytes_accessed=24 << 20, transcendentals=0),
    )(meta, parent_tiles, moved, *sa, *sb, *panel)


def per_device(
    contribution,
    parent_tiles,
    row_basis,
    pivot_basis,
    tile_ranks,
    block_map,
    panel_start,
    pivot_inverse,
):
    my_row = lax.axis_index("row")
    my_col = lax.axis_index("col")
    meta = jnp.concatenate(
        [block_map, tile_ranks, panel_start, jnp.stack([my_row, my_col])]
    ).astype(jnp.int32)
    shifts = [block_map[16 * u] - 32 * u for u in range(4)]
    start = panel_start[0]

    def move_row(u, *others):
        tiles = contribution[2 * u : 2 * u + 2, 0, 0 : u + 1, 0]
        return rotate(after(tiles, *others), "row", 8, shifts[u] & 7)

    def move_col(s, rows, *others):
        tiles = jnp.concatenate([rows[u][:, s] for u in range(s, 4)])
        return rotate(after(tiles, *others), "col", 16, shifts[s])

    pivots = gather_rows(pivot_basis[:, 0])
    panel_at = jnp.minimum((start + ((my_col - start) & 15)) >> 4, parent_tiles.shape[2] - 1)
    parent_panel = across_col(
        lax.dynamic_index_in_dim(parent_tiles[:, 0, :, 0], panel_at, axis=1, keepdims=False)
    )
    parts = products(meta, pivots)
    wa = scatter_sums(parts[0:4], lambda v, d: col_perm(v, 0, d), lambda v, d: col_perm(v, d, 0))
    wb = scatter_sums(parts[4:8], lambda v, d: col_perm(v, d, 0), lambda v, d: col_perm(v, 0, d))

    rows = [None] * 4
    rows[3] = move_row(3, pivots[3])
    bases = gather_rows(after(row_basis[:, 0], pivots[3]))
    rows[2] = move_row(2, parts[0])
    rows[1] = move_row(1, parts[0])
    rows[0] = move_row(0, parts[0])
    send = panel_send(meta, pivots, rows)
    got = across_col(send)
    cols = [None] * 4
    cols[3] = move_col(3, rows, send)
    cols[2] = move_col(2, rows, send)

    panel, sa, sb = panel_row(meta, bases, parent_panel, got, pivot_inverse)
    turn = []
    for r in range(8):
        for c in range(16):
            turn.append((16 * r + c, 16 * (c // 2) + 8 * (c % 2) + r))
    panel = lax.ppermute(panel, ("row", "col"), turn)
    ring_a = jnp.stack([sa] + [col_perm(sa, 0, d) for d in (1, 2, 3)])
    ring_b = jnp.stack([sb] + [col_perm(sb, d, 0) for d in (1, 2, 3)])
    panel = gather_rows(after(panel, ring_a, ring_b))
    cols[1] = move_col(1, rows, ring_a, ring_b)
    cols[0] = move_col(0, rows, ring_a, ring_b)
    sa = [ring_a] + [col_perm(ring_a, d, 0) for d in (1, 2, 3)]
    sb = [ring_b] + [col_perm(ring_b, 0, d) for d in (1, 2, 3)]
    moved = moved_tiles(meta, wa, wb, bases, cols)
    return trailing_update(meta, parent_tiles, moved, sa, sb, panel)


def solution(mesh):
    placed = (
        P(None, "row", None, "col", None, None),
        P(None, "row", None, "col", None, None),
        P(None, "row", None, None),
        P(None, "row", None, "col"),
        P(),
        P(),
        P(),
        P(),
    )
    return jax.shard_map(
        per_device,
        mesh=mesh,
        in_specs=placed,
        out_specs=P(None, "row", None, "col", None, None),
        check_vma=False,
    )
```

```python
import jax
import jax.numpy as jnp
from jax import lax
from jax.experimental import pallas as pl
from jax.experimental.pallas import tpu as pltpu
from jax.sharding import PartitionSpec as P

PANEL_T = 4
F32 = jnp.float32
BF16 = jnp.bfloat16


def shift_of(meta, u):
    return meta[16 * u] - 32 * u


def gathered_row(meta, k):
    row = meta[129]
    return 2 * (((row >> 1) - k % 4) & 3) + ((row + k // 4) & 1)


def row_source(meta, u):
    return (meta[129] - shift_of(meta, u)) & 7


def col_source(meta, s, col):
    return (col - shift_of(meta, s)) & 15


def panel_child(meta, p):
    tile = meta[128] + p
    s = tile >> 5
    at = tile - meta[16 * s]
    return s, at & 15, (at >= 0) & (at < 16)


def split2(x):
    hi = x.astype(BF16)
    return hi, (x - hi.astype(F32)).astype(BF16)


def dot3(a, b, dims):
    dn = (dims, ((), ()))
    ah, al = a
    bh, bl = b
    low = lax.dot_general(ah, bl, dn, preferred_element_type=F32)
    low += lax.dot_general(al, bh, dn, preferred_element_type=F32)
    return lax.dot_general(ah, bh, dn, preferred_element_type=F32) + low


NT = ((1,), (1,))
NN = ((1,), (0,))
TN = ((0,), (0,))


def after(x, *others):
    return lax.optimization_barrier((x,) + others)[0]


def row_perm(x, dy, dc):
    pairs = [(2 * y + k, 2 * ((y + dy) % 4) + (k + dc) % 2) for y in range(4) for k in range(2)]
    return lax.ppermute(x, "row", pairs)


def col_perm(x, dx, dz):
    pairs = [(4 * a + b, 4 * ((a + dx) % 4) + (b + dz) % 4) for a in range(4) for b in range(4)]
    return lax.ppermute(x, "col", pairs)


def gather_rows(x, *first):
    ring = [x] + [row_perm(x, d, 0) for d in (1, 2, 3)]
    return ring + [row_perm(v if k == 0 else after(v, *first), 0, 1) for k, v in enumerate(ring)]


def rotate(x, axis, count, by):
    def step(k):
        pairs = [(i, (i + k) % count) for i in range(count)]
        return (lambda v: lax.ppermute(v, axis, pairs)) if k else (lambda v: v)

    return lax.switch(by, [step(k) for k in range(count)], x)


def across_col(x):
    return lax.all_to_all(x, "col", split_axis=0, concat_axis=0, tiled=True)


def whole():
    return pl.BlockSpec(memory_space=pltpu.VMEM)


def products_kernel(meta, *refs):
    v_refs, out_ref = refs[0:8], refs[8]
    vh_ref, vl_ref, hi_ref, lo_ref, ph_ref, pl_ref = refs[9:15]
    e = pl.program_id(0)

    @pl.when(e == 0)
    def _():
        for k in range(8):
            rho = gathered_row(meta, k)
            hi, lo = split2(v_refs[k][...])
            vh_ref[rho] = hi
            vl_ref[rho] = lo
        for u in range(4):
            rho = row_source(meta, u)
            for w in range(2):
                at = 128 * u + 64 * w
                hi_ref[at : at + 64] = vh_ref[rho, 2 * u + w]
                lo_ref[at : at + 64] = vl_ref[rho, 2 * u + w]
        for p in range(PANEL_T):
            s, at, _ = panel_child(meta, p)
            ph_ref[64 * p : 64 * p + 64] = vh_ref[at & 7, 2 * s + (at >> 3)]
            pl_ref[64 * p : 64 * p + 64] = vl_ref[at & 7, 2 * s + (at >> 3)]

    def left(first, last):
        return hi_ref[first:last], lo_ref[first:last]

    def right(col, s, q):
        places = []
        for k in (s, q):
            j = col_source(meta, k, col)
            places.append((j & 7, 2 * k + (j >> 3)))
        return tuple(
            jnp.concatenate([ref[places[0]], ref[places[1]]], axis=0) for ref in (vh_ref, vl_ref)
        )

    low_half = lax.broadcasted_iota(jnp.int32, (128, 128), 1) < 64
    for d in range(4):
        other = 4 * e + d
        out_ref[d, 0:384] = dot3(left(128, 512), right(other, 0, 1), NT)
        ends = right(other, 0, 3)
        out_ref[d, 384:512] = jnp.where(
            low_half, dot3(left(0, 128), ends, NT), dot3(left(384, 512), ends, NT)
        )
        mid = right(other, 2, 2)
        out_ref[d, 512:640] = jnp.where(
            low_half, dot3(left(256, 384), mid, NT), dot3(left(384, 512), mid, NT)
        )
        at = (8 * other + meta[129] - meta[16 * e]) & 15
        mine = pl.ds(pl.multiple_of(128 * e + 64 * (at >> 3), 64), 64)
        own = (hi_ref[mine], lo_ref[mine])
        out_ref[d, 640:704] = dot3(own, (ph_ref[0:128], pl_ref[0:128]), NT)
        out_ref[d, 704:768] = dot3(own, (ph_ref[128:256], pl_ref[128:256]), NT)


def products(meta, pivots):
    return pl.pallas_call(
        products_kernel,
        grid_spec=pltpu.PrefetchScalarGridSpec(
            num_scalar_prefetch=1,
            grid=(4,),
            in_specs=[whole()] * 8,
            out_specs=pl.BlockSpec((4, 768, 128), lambda e, meta: (e, 0, 0)),
            scratch_shapes=[pltpu.VMEM((8, 8, 64, 128), BF16)] * 2
            + [pltpu.VMEM((512, 128), BF16)] * 2
            + [pltpu.VMEM((256, 128), BF16)] * 2,
        ),
        out_shape=jax.ShapeDtypeStruct((16, 768, 128), F32),
        compiler_params=pltpu.CompilerParams(vmem_limit_bytes=24 << 20),
        cost_estimate=pl.CostEstimate(flops=2 * 10**9, bytes_accessed=8 << 20, transcendentals=0),
    )(meta, *pivots)


def panel_block(meta):
    start, col = meta[128], meta[130]
    return jnp.minimum((start + ((col - start) & 15)) >> 4, 7)


def child_block(meta):
    mine = jnp.int32(0)
    for s in range(1, 4):
        p = meta[16 * s] + meta[130] - meta[128]
        mine = jnp.where((p >= 0) & (p < PANEL_T), s, mine)
    return mine


def pick_kernel(meta, parent_ref, *refs):
    c_refs, out_ref = refs[0:4], refs[4]
    mine = child_block(meta)
    for a in range(16):
        out_ref[a, 0] = parent_ref[a, 0, 0, 0]
    for u in range(4):
        for w in range(2):
            slot = (meta[16 * u] + 8 * w + row_source(meta, u)) >> 3
            out_ref[slot, 1] = c_refs[u][w, jnp.minimum(mine, u)]


def panel_pick(meta, parent_tiles, rows):
    return pl.pallas_call(
        pick_kernel,
        grid_spec=pltpu.PrefetchScalarGridSpec(
            num_scalar_prefetch=1,
            grid=(1,),
            in_specs=[
                pl.BlockSpec(
                    (16, 1, 1, 1, 128, 128), lambda i, meta: (0, 0, panel_block(meta), 0, 0, 0)
                )
            ]
            + [whole()] * 4,
            out_specs=whole(),
        ),
        out_shape=jax.ShapeDtypeStruct((16, 2, 128, 128), F32),
        compiler_params=pltpu.CompilerParams(vmem_limit_bytes=16 << 20),
        cost_estimate=pl.CostEstimate(flops=0, bytes_accessed=4 << 20, transcendentals=0),
    )(meta, parent_tiles, *rows)


def masked_basis(meta, ref, rho, t, tile):
    rows = lax.broadcasted_iota(jnp.int32, (64, 128), 0)
    return jnp.where(rows < meta[64 + tile], ref[rho, t], 0.0)


def block_diagonal(first, second):
    zero = jnp.zeros((64, 128), F32)
    top = jnp.concatenate([first, zero], axis=1)
    bottom = jnp.concatenate([zero, second], axis=1)
    return split2(jnp.concatenate([top, bottom], axis=0))


def panel_kernel(meta, w_ref, base_ref, got_ref, inverse_ref, panel_ref, sa_ref, sb_ref):
    row, col = meta[129], meta[130]
    u = col >> 2
    at = 8 * col + row - meta[16 * u]
    row_ok = (at >= 0) & (at < 16)
    at = at & 15
    tile = 16 * u + at
    bi = split2(masked_basis(meta, base_ref, at & 7, 2 * u + (at >> 3), tile))
    bj, keep, children = [], [], []
    for p in range(PANEL_T):
        s, at_col, col_ok = panel_child(meta, p)
        other = 16 * s + at_col
        bj.append(masked_basis(meta, base_ref, at_col & 7, 2 * s + (at_col >> 3), other))
        keep.append(row_ok & col_ok & (tile >= other))
        children.append(got_ref[at_col, 1])
    half = [
        dot3(split2(w_ref[0, 640:704]), block_diagonal(bj[0], bj[1]), NN),
        dot3(split2(w_ref[0, 704:768]), block_diagonal(bj[2], bj[3]), NN),
    ]
    update = dot3(bi, split2(jnp.concatenate(half, axis=1)), TN)
    tiles = []
    for p in range(PANEL_T):
        moved = children[p] - update[:, 128 * p : 128 * p + 128]
        tiles.append(got_ref[(meta[128] + p) & 15, 0] + jnp.where(keep[p], moved, 0.0))
    panel = jnp.concatenate(tiles, axis=1)
    panel_ref[...] = panel
    out = dot3(split2(panel), split2(inverse_ref[...]), NN)
    sa_ref[...] = out[0:64]
    sb_ref[...] = out[64:128]


def panel_row(meta, weights, bases, got, inverse):
    return pl.pallas_call(
        panel_kernel,
        grid_spec=pltpu.PrefetchScalarGridSpec(
            num_scalar_prefetch=1, grid=(), in_specs=[whole()] * 4, out_specs=[whole()] * 3
        ),
        out_shape=[
            jax.ShapeDtypeStruct((128, 512), F32),
            jax.ShapeDtypeStruct((64, 512), F32),
            jax.ShapeDtypeStruct((64, 512), F32),
        ],
        compiler_params=pltpu.CompilerParams(vmem_limit_bytes=32 << 20),
        cost_estimate=pl.CostEstimate(flops=4 * 10**8, bytes_accessed=6 << 20, transcendentals=0),
    )(meta, weights, bases, got, inverse)


def moved_kernel(meta, w_ref, base_ref, *refs):
    c_refs, out_ref, g_ref = refs[0:4], refs[4], refs[5]
    col = meta[130]
    bj = []
    for s in range(4):
        j = col_source(meta, s, col)
        bj.append(masked_basis(meta, base_ref, j & 7, 2 * s + (j >> 3), 16 * s + j))
    d01, d03, d22 = (block_diagonal(bj[s], bj[q]) for s, q in ((0, 1), (0, 3), (2, 2)))
    g_ref[0:384] = dot3(split2(w_ref[0, 0:384]), d01, NN)
    g_ref[384:512] = dot3(split2(w_ref[0, 384:512]), d03, NN)
    g_ref[512:640] = dot3(split2(w_ref[0, 512:640]), d22, NN)

    for t in range(8):
        u, w = t // 2, t % 2
        rho = row_source(meta, u)
        bi = split2(masked_basis(meta, base_ref, rho, t, 16 * u + 8 * w + rho))

        def put(s, tile):
            value = c_refs[s][2 * (u - s) + w] - tile
            if u == s:
                keep = rho + 8 * w >= col_source(meta, s, col)
                value = jnp.where(keep, value, 0.0)
            out_ref[u * (u + 1) + w * (u + 1) + s] = value

        def update(first, lane, wide):
            return dot3(bi, split2(g_ref[first : first + 64, lane : lane + wide]), TN)

        if t >= 2:
            both = update(64 * (t - 2), 0, 256)
            put(0, both[:, 0:128])
            put(1, both[:, 128:256])
        else:
            put(0, update(384 + 64 * t, 0, 128))
        if u == 2:
            put(2, update(512 + 64 * w, 0, 128))
        if u == 3:
            put(2, update(512 + 64 * w, 128, 128))
            put(3, update(384 + 64 * w, 128, 128))


def moved_tiles(meta, weights, bases, cols):
    return pl.pallas_call(
        moved_kernel,
        grid_spec=pltpu.PrefetchScalarGridSpec(
            num_scalar_prefetch=1,
            grid=(),
            in_specs=[whole()] * 6,
            out_specs=whole(),
            scratch_shapes=[pltpu.VMEM((640, 256), F32)],
        ),
        out_shape=jax.ShapeDtypeStruct((20, 128, 128), F32),
        compiler_params=pltpu.CompilerParams(vmem_limit_bytes=32 << 20),
        cost_estimate=pl.CostEstimate(flops=10**9, bytes_accessed=6 << 20, transcendentals=0),
    )(meta, weights, bases, *cols)


def trailing_kernel(meta, parent_ref, moved_ref, *refs):
    a_refs, b_refs, panel_refs, out_ref = refs[0:4], refs[4:8], refs[8:12], refs[12]
    s_ref, p_ref = refs[13:15]
    q, g = pl.program_id(0), pl.program_id(1)
    row, col, start = meta[129], meta[130], meta[128]
    x, z = col >> 2, col & 3

    @pl.when((q == 0) & (g == 0))
    def _():
        for k in range(8):
            tile = gathered_row(meta, k)
            hi, lo = split2(panel_refs[k % 4][k // 4])
            p_ref[tile >> 1, tile & 1] = jnp.concatenate([hi, hi, lo], axis=1)
        for m in range(4):
            for n in range(4):
                hi, lo = split2(a_refs[m][n])
                s_ref[(x - m) & 3, (z - n) & 3, 0:64] = jnp.concatenate([hi, lo, hi], axis=1)
                hi, lo = split2(b_refs[m][n])
                s_ref[(x - n) & 3, (z - m) & 3, 64:128] = jnp.concatenate([hi, lo, hi], axis=1)

    def assembled(k, j):
        tile_row = 8 * (4 * g + k) + row
        tile_col = 16 * (2 * q + j) + col
        at = tile_row - meta[16 * g]
        at_col = tile_col - meta[16 * q]
        use = (at >= 0) & (at < 16) & (at_col >= 0) & (at_col < 16) & (g >= q)
        index = jnp.where(use, g * (g + 1) + (at >> 3) * (g + 1) + q, 0)
        tile = parent_ref[k, 0, j, 0] + jnp.where(use, moved_ref[index], 0.0)
        return tile, (tile_row >= tile_col) & (tile_col >= start + PANEL_T)

    first_col = 32 * q + col
    active = (32 * g + 24 + row >= first_col) & (first_col + 16 >= start + PANEL_T)

    @pl.when(active)
    def _():
        left, right = s_ref[g].reshape(512, 1536), p_ref[q].reshape(256, 1536)
        trailing = lax.dot_general(left, right, (NT, ((), ())), preferred_element_type=F32)
        for k in range(4):
            for j in range(2):
                tile, window = assembled(k, j)
                part = trailing[128 * k : 128 * k + 128, 128 * j : 128 * j + 128]
                out_ref[k, 0, j, 0] = tile - jnp.where(window, part, 0.0)

    @pl.when(jnp.logical_not(active))
    def _():
        for k in range(4):
            for j in range(2):
                out_ref[k, 0, j, 0] = assembled(k, j)[0]


def trailing_update(meta, parent_tiles, moved, sa, sb, panel):
    tiles = pl.BlockSpec((4, 1, 2, 1, 128, 128), lambda q, g, meta: (g, 0, q, 0, 0, 0))
    return pl.pallas_call(
        trailing_kernel,
        grid_spec=pltpu.PrefetchScalarGridSpec(
            num_scalar_prefetch=1,
            grid=(4, 4),
            in_specs=[tiles] + [whole()] * 13,
            out_specs=tiles,
            scratch_shapes=[
                pltpu.VMEM((4, 4, 128, 1536), BF16),
                pltpu.VMEM((4, 2, 128, 1536), BF16),
            ],
        ),
        out_shape=jax.ShapeDtypeStruct(parent_tiles.shape, F32),
        compiler_params=pltpu.CompilerParams(vmem_limit_bytes=40 << 20),
        cost_estimate=pl.CostEstimate(flops=7 * 10**9, bytes_accessed=24 << 20, transcendentals=0),
    )(meta, parent_tiles, moved, *sa, *sb, *panel)


def per_device(
    contribution,
    parent_tiles,
    row_basis,
    pivot_basis,
    tile_ranks,
    block_map,
    panel_start,
    pivot_inverse,
):
    my_row = lax.axis_index("row")
    my_col = lax.axis_index("col")
    meta = jnp.concatenate(
        [block_map, tile_ranks, panel_start, jnp.stack([my_row, my_col])]
    ).astype(jnp.int32)
    shifts = [block_map[16 * u] - 32 * u for u in range(4)]

    last = rotate(contribution[6:, 0, 3, 0], "col", 16, shifts[3])
    tiles = [contribution[2 * u : 2 * u + 2, 0, 0 : u + 1, 0] for u in range(3)]
    tiles.append(jnp.concatenate([contribution[6:, 0, 0:3, 0], last[:, None]], axis=1))
    pivots = gather_rows(pivot_basis[:, 0], *tiles)
    parts = products(meta, pivots)
    weights = lax.psum_scatter(parts, "col", scatter_dimension=0, tiled=True)
    rows = [rotate(after(tiles[u], parts), "row", 8, shifts[u] & 7) for u in range(4)]
    picked = panel_pick(meta, parent_tiles, rows)
    got = across_col(picked)
    bases = lax.all_gather(after(row_basis[:, 0], picked), "row", axis=0)
    cols = [
        rotate(
            after(jnp.concatenate([rows[u][:, s] for u in range(s, 4)]), picked),
            "col",
            16,
            shifts[s],
        )
        for s in range(3)
    ]
    cols.append(rows[3][:, 3])
    panel, sa, sb = panel_row(meta, after(weights, *cols), bases, got, pivot_inverse)
    turn = []
    for r in range(8):
        for c in range(16):
            turn.append((16 * r + c, 16 * (c // 2) + 8 * (c % 2) + r))
    panel = lax.ppermute(panel, ("row", "col"), turn)
    ring_a = jnp.stack([sa] + [col_perm(sa, 0, d) for d in (1, 2, 3)])
    ring_b = jnp.stack([sb] + [col_perm(sb, d, 0) for d in (1, 2, 3)])
    sa = [ring_a] + [col_perm(ring_a, d, 0) for d in (1, 2, 3)]
    sb = [ring_b] + [col_perm(ring_b, 0, d) for d in (1, 2, 3)]
    panel = jnp.stack([panel, row_perm(panel, 0, 1)])
    panel = [panel] + [row_perm(panel, d, 0) for d in (1, 2, 3)]
    moved = moved_tiles(meta, weights, bases, cols)
    return trailing_update(meta, parent_tiles, moved, sa, sb, panel)


def solution(mesh):
    placed = (
        P(None, "row", None, "col", None, None),
        P(None, "row", None, "col", None, None),
        P(None, "row", None, None),
        P(None, "row", None, "col"),
        P(),
        P(),
        P(),
        P(),
    )
    return jax.shard_map(
        per_device,
        mesh=mesh,
        in_specs=placed,
        out_specs=P(None, "row", None, "col", None, None),
        check_vma=False,
    )
```

```python
import jax
import jax.numpy as jnp
from jax import lax
from jax.experimental import pallas as pl
from jax.experimental.pallas import tpu as pltpu
from jax.sharding import PartitionSpec as P

PANEL_T = 4
F32 = jnp.float32
BF16 = jnp.bfloat16


def shift_of(meta, u):
    return meta[16 * u] - 32 * u


def gathered_row(meta, k):
    row = meta[129]
    return 2 * (((row >> 1) - k % 4) & 3) + ((row + k // 4) & 1)


def row_source(meta, u):
    return (meta[129] - shift_of(meta, u)) & 7


def col_source(meta, s, col):
    return (col - shift_of(meta, s)) & 15


def panel_child(meta, p):
    tile = meta[128] + p
    s = tile >> 5
    at = tile - meta[16 * s]
    return s, at & 15, (at >= 0) & (at < 16)


def split2(x):
    hi = x.astype(BF16)
    return hi, (x - hi.astype(F32)).astype(BF16)


def dot3(a, b, dims):
    dn = (dims, ((), ()))
    ah, al = a
    bh, bl = b
    low = lax.dot_general(ah, bl, dn, preferred_element_type=F32)
    low += lax.dot_general(al, bh, dn, preferred_element_type=F32)
    return lax.dot_general(ah, bh, dn, preferred_element_type=F32) + low


NT = ((1,), (1,))
NN = ((1,), (0,))
TN = ((0,), (0,))


def after(x, *others):
    return lax.optimization_barrier((x,) + others)[0]


def row_perm(x, dy, dc):
    pairs = [(2 * y + k, 2 * ((y + dy) % 4) + (k + dc) % 2) for y in range(4) for k in range(2)]
    return lax.ppermute(x, "row", pairs)


def col_perm(x, dx, dz):
    pairs = [(4 * a + b, 4 * ((a + dx) % 4) + (b + dz) % 4) for a in range(4) for b in range(4)]
    return lax.ppermute(x, "col", pairs)


def gather_rows(x, *first):
    ring = [x] + [row_perm(x, d, 0) for d in (1, 2, 3)]
    return ring + [row_perm(v if k == 0 else after(v, *first), 0, 1) for k, v in enumerate(ring)]


def rotate(x, axis, count, by):
    def step(k):
        pairs = [(i, (i + k) % count) for i in range(count)]
        return (lambda v: lax.ppermute(v, axis, pairs)) if k else (lambda v: v)

    return lax.switch(by, [step(k) for k in range(count)], x)


def across_col(x):
    return lax.all_to_all(x, "col", split_axis=0, concat_axis=0, tiled=True)


def whole():
    return pl.BlockSpec(memory_space=pltpu.VMEM)


def products_kernel(meta, *refs):
    v_refs, out_ref = refs[0:8], refs[8]
    vh_ref, vl_ref, hi_ref, lo_ref, ph_ref, pl_ref = refs[9:15]
    e = pl.program_id(0)

    @pl.when(e == 0)
    def _():
        for k in range(8):
            rho = gathered_row(meta, k)
            hi, lo = split2(v_refs[k][...])
            vh_ref[rho] = hi
            vl_ref[rho] = lo
        for u in range(4):
            rho = row_source(meta, u)
            for w in range(2):
                at = 128 * u + 64 * w
                hi_ref[at : at + 64] = vh_ref[rho, 2 * u + w]
                lo_ref[at : at + 64] = vl_ref[rho, 2 * u + w]
        for p in range(PANEL_T):
            s, at, _ = panel_child(meta, p)
            ph_ref[64 * p : 64 * p + 64] = vh_ref[at & 7, 2 * s + (at >> 3)]
            pl_ref[64 * p : 64 * p + 64] = vl_ref[at & 7, 2 * s + (at >> 3)]

    def left(first, last):
        return hi_ref[first:last], lo_ref[first:last]

    def right(col, s, q):
        places = []
        for k in (s, q):
            j = col_source(meta, k, col)
            places.append((j & 7, 2 * k + (j >> 3)))
        return tuple(
            jnp.concatenate([ref[places[0]], ref[places[1]]], axis=0) for ref in (vh_ref, vl_ref)
        )

    low_half = lax.broadcasted_iota(jnp.int32, (128, 128), 1) < 64
    for d in range(4):
        other = 4 * e + d
        out_ref[d, 0:384] = dot3(left(128, 512), right(other, 0, 1), NT)
        ends = right(other, 0, 3)
        out_ref[d, 384:512] = jnp.where(
            low_half, dot3(left(0, 128), ends, NT), dot3(left(384, 512), ends, NT)
        )
        mid = right(other, 2, 2)
        out_ref[d, 512:640] = jnp.where(
            low_half, dot3(left(256, 384), mid, NT), dot3(left(384, 512), mid, NT)
        )
        at = (8 * other + meta[129] - meta[16 * e]) & 15
        mine = pl.ds(pl.multiple_of(128 * e + 64 * (at >> 3), 64), 64)
        own = (hi_ref[mine], lo_ref[mine])
        out_ref[d, 640:704] = dot3(own, (ph_ref[0:128], pl_ref[0:128]), NT)
        out_ref[d, 704:768] = dot3(own, (ph_ref[128:256], pl_ref[128:256]), NT)


def products(meta, pivots):
    return pl.pallas_call(
        products_kernel,
        grid_spec=pltpu.PrefetchScalarGridSpec(
            num_scalar_prefetch=1,
            grid=(4,),
            in_specs=[whole()] * 8,
            out_specs=pl.BlockSpec((4, 768, 128), lambda e, meta: (e, 0, 0)),
            scratch_shapes=[pltpu.VMEM((8, 8, 64, 128), BF16)] * 2
            + [pltpu.VMEM((512, 128), BF16)] * 2
            + [pltpu.VMEM((256, 128), BF16)] * 2,
        ),
        out_shape=jax.ShapeDtypeStruct((16, 768, 128), F32),
        compiler_params=pltpu.CompilerParams(vmem_limit_bytes=60 << 20),
        cost_estimate=pl.CostEstimate(flops=2 * 10**9, bytes_accessed=8 << 20, transcendentals=0),
    )(meta, *pivots)


def panel_block(meta):
    start, col = meta[128], meta[130]
    return jnp.minimum((start + ((col - start) & 15)) >> 4, 7)


def child_block(meta):
    mine = jnp.int32(0)
    for s in range(1, 4):
        p = meta[16 * s] + meta[130] - meta[128]
        mine = jnp.where((p >= 0) & (p < PANEL_T), s, mine)
    return mine


def pick_kernel(meta, parent_ref, *refs):
    c_refs, out_ref = refs[0:4], refs[4]
    mine = child_block(meta)
    for a in range(16):
        out_ref[a, 0] = parent_ref[a, 0, 0, 0]
    for u in range(4):
        for w in range(2):
            slot = (meta[16 * u] + 8 * w + row_source(meta, u)) >> 3
            out_ref[slot, 1] = c_refs[u][w, jnp.minimum(mine, u)]


def panel_pick(meta, parent_tiles, rows):
    return pl.pallas_call(
        pick_kernel,
        grid_spec=pltpu.PrefetchScalarGridSpec(
            num_scalar_prefetch=1,
            grid=(1,),
            in_specs=[
                pl.BlockSpec(
                    (16, 1, 1, 1, 128, 128), lambda i, meta: (0, 0, panel_block(meta), 0, 0, 0)
                )
            ]
            + [whole()] * 4,
            out_specs=whole(),
        ),
        out_shape=jax.ShapeDtypeStruct((16, 2, 128, 128), F32),
        compiler_params=pltpu.CompilerParams(vmem_limit_bytes=60 << 20),
        cost_estimate=pl.CostEstimate(flops=0, bytes_accessed=4 << 20, transcendentals=0),
    )(meta, parent_tiles, *rows)


def masked_basis(meta, ref, rho, t, tile):
    rows = lax.broadcasted_iota(jnp.int32, (64, 128), 0)
    return jnp.where(rows < meta[64 + tile], ref[rho, t], 0.0)


def block_diagonal(first, second):
    zero = jnp.zeros((64, 128), F32)
    top = jnp.concatenate([first, zero], axis=1)
    bottom = jnp.concatenate([zero, second], axis=1)
    return split2(jnp.concatenate([top, bottom], axis=0))


def panel_kernel(meta, w_ref, base_ref, got_ref, inverse_ref, panel_ref, sa_ref, sb_ref):
    row, col = meta[129], meta[130]
    u = col >> 2
    at = 8 * col + row - meta[16 * u]
    row_ok = (at >= 0) & (at < 16)
    at = at & 15
    tile = 16 * u + at
    bi = split2(masked_basis(meta, base_ref, at & 7, 2 * u + (at >> 3), tile))
    bj, keep, children = [], [], []
    for p in range(PANEL_T):
        s, at_col, col_ok = panel_child(meta, p)
        other = 16 * s + at_col
        bj.append(masked_basis(meta, base_ref, at_col & 7, 2 * s + (at_col >> 3), other))
        keep.append(row_ok & col_ok & (tile >= other))
        children.append(got_ref[at_col, 1])
    half = [
        dot3(split2(w_ref[0, 640:704]), block_diagonal(bj[0], bj[1]), NN),
        dot3(split2(w_ref[0, 704:768]), block_diagonal(bj[2], bj[3]), NN),
    ]
    update = dot3(bi, split2(jnp.concatenate(half, axis=1)), TN)
    tiles = []
    for p in range(PANEL_T):
        moved = children[p] - update[:, 128 * p : 128 * p + 128]
        tiles.append(got_ref[(meta[128] + p) & 15, 0] + jnp.where(keep[p], moved, 0.0))
    panel = jnp.concatenate(tiles, axis=1)
    panel_ref[...] = panel
    out = dot3(split2(panel), split2(inverse_ref[...]), NN)
    sa_ref[...] = out[0:64]
    sb_ref[...] = out[64:128]


def panel_row(meta, weights, bases, got, inverse):
    return pl.pallas_call(
        panel_kernel,
        grid_spec=pltpu.PrefetchScalarGridSpec(
            num_scalar_prefetch=1, grid=(), in_specs=[whole()] * 4, out_specs=[whole()] * 3
        ),
        out_shape=[
            jax.ShapeDtypeStruct((128, 512), F32),
            jax.ShapeDtypeStruct((64, 512), F32),
            jax.ShapeDtypeStruct((64, 512), F32),
        ],
        compiler_params=pltpu.CompilerParams(vmem_limit_bytes=32 << 20),
        cost_estimate=pl.CostEstimate(flops=4 * 10**8, bytes_accessed=6 << 20, transcendentals=0),
    )(meta, weights, bases, got, inverse)


def moved_kernel(meta, w_ref, base_ref, *refs):
    c_refs, parent_ref, all_ref, g_ref, out_ref = refs[0:4], refs[4], refs[5], refs[6], refs[7]
    col = meta[130]
    bj = []
    for s in range(4):
        j = col_source(meta, s, col)
        bj.append(masked_basis(meta, base_ref, j & 7, 2 * s + (j >> 3), 16 * s + j))
    d01, d03, d22 = (block_diagonal(bj[s], bj[q]) for s, q in ((0, 1), (0, 3), (2, 2)))
    g_ref[0:384] = dot3(split2(w_ref[0, 0:384]), d01, NN)
    g_ref[384:512] = dot3(split2(w_ref[0, 384:512]), d03, NN)
    g_ref[512:640] = dot3(split2(w_ref[0, 512:640]), d22, NN)

    for t in range(8):
        u, w = t // 2, t % 2
        rho = row_source(meta, u)
        bi = split2(masked_basis(meta, base_ref, rho, t, 16 * u + 8 * w + rho))

        def put(s, tile):
            value = c_refs[s][2 * (u - s) + w] - tile
            if u == s:
                keep = rho + 8 * w >= col_source(meta, s, col)
                value = jnp.where(keep, value, 0.0)
            out_ref[u * (u + 1) + w * (u + 1) + s] = value

        def update(first, lane, wide):
            return dot3(bi, split2(g_ref[first : first + 64, lane : lane + wide]), TN)

        if t >= 2:
            both = update(64 * (t - 2), 0, 256)
            put(0, both[:, 0:128])
            put(1, both[:, 128:256])
        else:
            put(0, update(384 + 64 * t, 0, 128))
        if u == 2:
            put(2, update(512 + 64 * w, 0, 128))
        if u == 3:
            put(2, update(512 + 64 * w, 128, 128))
            put(3, update(384 + 64 * w, 128, 128))


    row = meta[129]

    def assemble(a, carry):
        u = a >> 2
        at = 8 * a + row - meta[16 * u]
        for b in range(8):
            s = b // 2
            at_col = 16 * b + col - meta[16 * s]
            use = (at >= 0) & (at < 16) & (at_col >= 0) & (at_col < 16) & (u >= s)
            index = jnp.where(use, u * (u + 1) + (at >> 3) * (u + 1) + s, 0)
            all_ref[a, b] = parent_ref[a, 0, b, 0] + jnp.where(use, out_ref[index], 0.0)
        return carry

    lax.fori_loop(0, 16, assemble, 0)


def assembled_tiles(meta, weights, bases, cols, parent_tiles):
    return pl.pallas_call(
        moved_kernel,
        grid_spec=pltpu.PrefetchScalarGridSpec(
            num_scalar_prefetch=1,
            grid=(),
            in_specs=[whole()] * 7,
            out_specs=whole(),
            scratch_shapes=[pltpu.VMEM((640, 256), F32), pltpu.VMEM((20, 128, 128), F32)],
        ),
        out_shape=jax.ShapeDtypeStruct((16, 8, 128, 128), F32),
        compiler_params=pltpu.CompilerParams(vmem_limit_bytes=24 << 20),
        cost_estimate=pl.CostEstimate(flops=10**9, bytes_accessed=16 << 20, transcendentals=0),
    )(meta, weights, bases, *cols, parent_tiles)


def trailing_kernel(meta, all_ref, *refs):
    a_refs, b_refs, panel_refs, out_ref = refs[0:4], refs[4:8], refs[8:12], refs[12]
    s_ref, p_ref = refs[13:15]
    q, g = pl.program_id(0), pl.program_id(1)
    row, col, start = meta[129], meta[130], meta[128]
    x, z = col >> 2, col & 3

    @pl.when((q == 0) & (g == 0))
    def _():
        for k in range(8):
            tile = gathered_row(meta, k)
            hi, lo = split2(panel_refs[k % 4][k // 4])
            p_ref[tile >> 1, tile & 1] = jnp.concatenate([hi, hi, lo], axis=1)
        for m in range(4):
            for n in range(4):
                hi, lo = split2(a_refs[m][n])
                s_ref[(x - m) & 3, (z - n) & 3, 0:64] = jnp.concatenate([hi, lo, hi], axis=1)
                hi, lo = split2(b_refs[m][n])
                s_ref[(x - n) & 3, (z - m) & 3, 64:128] = jnp.concatenate([hi, lo, hi], axis=1)

    def window(k, j):
        tile_row = 8 * (4 * g + k) + row
        tile_col = 16 * (2 * q + j) + col
        return (tile_row >= tile_col) & (tile_col >= start + PANEL_T)

    first_col = 32 * q + col
    active = (32 * g + 24 + row >= first_col) & (first_col + 16 >= start + PANEL_T)

    @pl.when(active)
    def _():
        left, right = s_ref[g].reshape(512, 1536), p_ref[q].reshape(256, 1536)
        trailing = lax.dot_general(left, right, (NT, ((), ())), preferred_element_type=F32)
        for k in range(4):
            for j in range(2):
                part = trailing[128 * k : 128 * k + 128, 128 * j : 128 * j + 128]
                tile = all_ref[4 * g + k, 2 * q + j]
                out_ref[k, 0, j, 0] = tile - jnp.where(window(k, j), part, 0.0)

    @pl.when(jnp.logical_not(active))
    def _():
        for k in range(4):
            for j in range(2):
                out_ref[k, 0, j, 0] = all_ref[4 * g + k, 2 * q + j]


def trailing_update(meta, assembled, shape, sa, sb, panel):
    tiles = pl.BlockSpec((4, 1, 2, 1, 128, 128), lambda q, g, meta: (g, 0, q, 0, 0, 0))
    return pl.pallas_call(
        trailing_kernel,
        grid_spec=pltpu.PrefetchScalarGridSpec(
            num_scalar_prefetch=1,
            grid=(4, 4),
            in_specs=[whole()] * 13,
            out_specs=tiles,
            scratch_shapes=[
                pltpu.VMEM((4, 4, 128, 1536), BF16),
                pltpu.VMEM((4, 2, 128, 1536), BF16),
            ],
        ),
        out_shape=jax.ShapeDtypeStruct(shape, F32),
        compiler_params=pltpu.CompilerParams(vmem_limit_bytes=24 << 20),
        cost_estimate=pl.CostEstimate(flops=7 * 10**9, bytes_accessed=24 << 20, transcendentals=0),
    )(meta, assembled, *sa, *sb, *panel)


def per_device(
    contribution,
    parent_tiles,
    row_basis,
    pivot_basis,
    tile_ranks,
    block_map,
    panel_start,
    pivot_inverse,
):
    my_row = lax.axis_index("row")
    my_col = lax.axis_index("col")
    meta = jnp.concatenate(
        [block_map, tile_ranks, panel_start, jnp.stack([my_row, my_col])]
    ).astype(jnp.int32)
    shifts = [block_map[16 * u] - 32 * u for u in range(4)]

    last = rotate(contribution[6:, 0, 3, 0], "col", 16, shifts[3])
    tiles = [contribution[2 * u : 2 * u + 2, 0, 0 : u + 1, 0] for u in range(3)]
    tiles.append(jnp.concatenate([contribution[6:, 0, 0:3, 0], last[:, None]], axis=1))
    pivots = gather_rows(pivot_basis[:, 0], *tiles)
    parts = products(meta, pivots)
    weights = lax.psum_scatter(parts, "col", scatter_dimension=0, tiled=True)
    rows = [rotate(after(tiles[u], parts), "row", 8, shifts[u] & 7) for u in range(4)]
    picked = panel_pick(meta, parent_tiles, rows)
    got = across_col(picked)
    bases = lax.all_gather(after(row_basis[:, 0], picked), "row", axis=0)
    cols = [
        rotate(
            after(jnp.concatenate([rows[u][:, s] for u in range(s, 4)]), picked),
            "col",
            16,
            shifts[s],
        )
        for s in range(3)
    ]
    cols.append(rows[3][:, 3])
    panel, sa, sb = panel_row(meta, after(weights, *cols), bases, got, pivot_inverse)
    turn = []
    for r in range(8):
        for c in range(16):
            turn.append((16 * r + c, 16 * (c // 2) + 8 * (c % 2) + r))
    panel = lax.ppermute(panel, ("row", "col"), turn)
    ring_a = jnp.stack([sa] + [col_perm(sa, 0, d) for d in (1, 2, 3)])
    ring_b = jnp.stack([sb] + [col_perm(sb, d, 0) for d in (1, 2, 3)])
    swapped = row_perm(panel, 0, 1)
    late_a, late_b = after(ring_a, swapped), after(ring_b, swapped)
    sa = [ring_a] + [col_perm(late_a if d == 2 else ring_a, d, 0) for d in (1, 2, 3)]
    sb = [ring_b] + [col_perm(late_b if d == 2 else ring_b, 0, d) for d in (1, 2, 3)]
    panel = jnp.stack([panel, swapped])
    panel = [panel] + [row_perm(panel, d, 0) for d in (1, 2, 3)]
    assembled = assembled_tiles(meta, weights, bases, cols, parent_tiles)
    return trailing_update(meta, assembled, parent_tiles.shape, sa, sb, panel)


def solution(mesh):
    placed = (
        P(None, "row", None, "col", None, None),
        P(None, "row", None, "col", None, None),
        P(None, "row", None, None),
        P(None, "row", None, "col"),
        P(),
        P(),
        P(),
        P(),
    )
    return jax.shard_map(
        per_device,
        mesh=mesh,
        in_specs=placed,
        out_specs=P(None, "row", None, "col", None, None),
        check_vma=False,
    )
```

```python
import jax
import jax.numpy as jnp
from jax import lax
from jax.experimental import pallas as pl
from jax.experimental.pallas import tpu as pltpu
from jax.sharding import PartitionSpec as P

PANEL_T = 4
F32 = jnp.float32
BF16 = jnp.bfloat16


def shift_of(meta, u):
    return meta[16 * u] - 32 * u


def gathered_row(meta, k):
    row = meta[129]
    return 2 * (((row >> 1) - k % 4) & 3) + ((row + k // 4) & 1)


def row_source(meta, u):
    return (meta[129] - shift_of(meta, u)) & 7


def col_source(meta, s, col):
    return (col - shift_of(meta, s)) & 15


def panel_child(meta, p):
    tile = meta[128] + p
    s = tile >> 5
    at = tile - meta[16 * s]
    return s, at & 15, (at >= 0) & (at < 16)


def split2(x):
    hi = x.astype(BF16)
    return hi, (x - hi.astype(F32)).astype(BF16)


def dot3(a, b, dims):
    dn = (dims, ((), ()))
    ah, al = a
    bh, bl = b
    low = lax.dot_general(ah, bl, dn, preferred_element_type=F32)
    low += lax.dot_general(al, bh, dn, preferred_element_type=F32)
    return lax.dot_general(ah, bh, dn, preferred_element_type=F32) + low


NT = ((1,), (1,))
NN = ((1,), (0,))
TN = ((0,), (0,))


def after(x, *others):
    return lax.optimization_barrier((x,) + others)[0]


def row_perm(x, dy, dc):
    pairs = [(2 * y + k, 2 * ((y + dy) % 4) + (k + dc) % 2) for y in range(4) for k in range(2)]
    return lax.ppermute(x, "row", pairs)


def col_perm(x, dx, dz):
    pairs = [(4 * a + b, 4 * ((a + dx) % 4) + (b + dz) % 4) for a in range(4) for b in range(4)]
    return lax.ppermute(x, "col", pairs)


def gather_rows(x, *first):
    ring = [x] + [row_perm(x, d, 0) for d in (1, 2, 3)]
    return ring + [row_perm(v if k == 0 else after(v, *first), 0, 1) for k, v in enumerate(ring)]


def rotate(x, axis, count, by):
    def step(k):
        pairs = [(i, (i + k) % count) for i in range(count)]
        return (lambda v: lax.ppermute(v, axis, pairs)) if k else (lambda v: v)

    return lax.switch(by, [step(k) for k in range(count)], x)


def across_col(x):
    return lax.all_to_all(x, "col", split_axis=0, concat_axis=0, tiled=True)


def whole():
    return pl.BlockSpec(memory_space=pltpu.VMEM)


def products_kernel(meta, *refs):
    v_refs, out_ref = refs[0:8], refs[8]
    vh_ref, vl_ref, hi_ref, lo_ref, ph_ref, pl_ref = refs[9:15]
    e = pl.program_id(0)

    @pl.when(e == 0)
    def _():
        for k in range(8):
            rho = gathered_row(meta, k)
            hi, lo = split2(v_refs[k][...])
            vh_ref[rho] = hi
            vl_ref[rho] = lo
        for u in range(4):
            rho = row_source(meta, u)
            for w in range(2):
                at = 128 * u + 64 * w
                hi_ref[at : at + 64] = vh_ref[rho, 2 * u + w]
                lo_ref[at : at + 64] = vl_ref[rho, 2 * u + w]
        for p in range(PANEL_T):
            s, at, _ = panel_child(meta, p)
            ph_ref[64 * p : 64 * p + 64] = vh_ref[at & 7, 2 * s + (at >> 3)]
            pl_ref[64 * p : 64 * p + 64] = vl_ref[at & 7, 2 * s + (at >> 3)]

    def left(first, last):
        return hi_ref[first:last], lo_ref[first:last]

    def right(col, s, q):
        places = []
        for k in (s, q):
            j = col_source(meta, k, col)
            places.append((j & 7, 2 * k + (j >> 3)))
        return tuple(
            jnp.concatenate([ref[places[0]], ref[places[1]]], axis=0) for ref in (vh_ref, vl_ref)
        )

    low_half = lax.broadcasted_iota(jnp.int32, (128, 128), 1) < 64
    for d in range(4):
        other = 4 * e + d
        out_ref[d, 0:384] = dot3(left(128, 512), right(other, 0, 1), NT)
        ends = right(other, 0, 3)
        out_ref[d, 384:512] = jnp.where(
            low_half, dot3(left(0, 128), ends, NT), dot3(left(384, 512), ends, NT)
        )
        mid = right(other, 2, 2)
        out_ref[d, 512:640] = jnp.where(
            low_half, dot3(left(256, 384), mid, NT), dot3(left(384, 512), mid, NT)
        )
        at = (8 * other + meta[129] - meta[16 * e]) & 15
        mine = pl.ds(pl.multiple_of(128 * e + 64 * (at >> 3), 64), 64)
        own = (hi_ref[mine], lo_ref[mine])
        out_ref[d, 640:704] = dot3(own, (ph_ref[0:128], pl_ref[0:128]), NT)
        out_ref[d, 704:768] = dot3(own, (ph_ref[128:256], pl_ref[128:256]), NT)


def products(meta, pivots):
    return pl.pallas_call(
        products_kernel,
        grid_spec=pltpu.PrefetchScalarGridSpec(
            num_scalar_prefetch=1,
            grid=(4,),
            in_specs=[whole()] * 8,
            out_specs=pl.BlockSpec((4, 768, 128), lambda e, meta: (e, 0, 0)),
            scratch_shapes=[pltpu.VMEM((8, 8, 64, 128), BF16)] * 2
            + [pltpu.VMEM((512, 128), BF16)] * 2
            + [pltpu.VMEM((256, 128), BF16)] * 2,
        ),
        out_shape=jax.ShapeDtypeStruct((16, 768, 128), F32),
        compiler_params=pltpu.CompilerParams(vmem_limit_bytes=60 << 20),
        cost_estimate=pl.CostEstimate(flops=2 * 10**9, bytes_accessed=8 << 20, transcendentals=0),
    )(meta, *pivots)


def panel_block(meta):
    start, col = meta[128], meta[130]
    return jnp.minimum((start + ((col - start) & 15)) >> 4, 7)


def child_block(meta):
    mine = jnp.int32(0)
    for s in range(1, 4):
        p = meta[16 * s] + meta[130] - meta[128]
        mine = jnp.where((p >= 0) & (p < PANEL_T), s, mine)
    return mine


def pick_kernel(meta, parent_ref, *refs):
    c_refs, out_ref = refs[0:4], refs[4]
    mine = child_block(meta)
    for a in range(16):
        out_ref[a, 0] = parent_ref[a, 0, 0, 0]
    for u in range(4):
        for w in range(2):
            slot = (meta[16 * u] + 8 * w + row_source(meta, u)) >> 3
            out_ref[slot, 1] = c_refs[u][w, jnp.minimum(mine, u)]


def panel_pick(meta, parent_tiles, rows):
    return pl.pallas_call(
        pick_kernel,
        grid_spec=pltpu.PrefetchScalarGridSpec(
            num_scalar_prefetch=1,
            grid=(1,),
            in_specs=[
                pl.BlockSpec(
                    (16, 1, 1, 1, 128, 128), lambda i, meta: (0, 0, panel_block(meta), 0, 0, 0)
                )
            ]
            + [whole()] * 4,
            out_specs=whole(),
        ),
        out_shape=jax.ShapeDtypeStruct((16, 2, 128, 128), F32),
        compiler_params=pltpu.CompilerParams(vmem_limit_bytes=60 << 20),
        cost_estimate=pl.CostEstimate(flops=0, bytes_accessed=4 << 20, transcendentals=0),
    )(meta, parent_tiles, *rows)


def masked_basis(meta, ref, rho, t, tile):
    rows = lax.broadcasted_iota(jnp.int32, (64, 128), 0)
    return jnp.where(rows < meta[64 + tile], ref[rho, t], 0.0)


def block_diagonal(first, second):
    zero = jnp.zeros((64, 128), F32)
    top = jnp.concatenate([first, zero], axis=1)
    bottom = jnp.concatenate([zero, second], axis=1)
    return split2(jnp.concatenate([top, bottom], axis=0))


def panel_kernel(meta, w_ref, base_ref, got_ref, inverse_ref, panel_ref, sa_ref, sb_ref):
    row, col = meta[129], meta[130]
    u = col >> 2
    at = 8 * col + row - meta[16 * u]
    row_ok = (at >= 0) & (at < 16)
    at = at & 15
    tile = 16 * u + at
    bi = split2(masked_basis(meta, base_ref, at & 7, 2 * u + (at >> 3), tile))
    bj, keep, children = [], [], []
    for p in range(PANEL_T):
        s, at_col, col_ok = panel_child(meta, p)
        other = 16 * s + at_col
        bj.append(masked_basis(meta, base_ref, at_col & 7, 2 * s + (at_col >> 3), other))
        keep.append(row_ok & col_ok & (tile >= other))
        children.append(got_ref[at_col, 1])
    half = [
        dot3(split2(w_ref[0, 640:704]), block_diagonal(bj[0], bj[1]), NN),
        dot3(split2(w_ref[0, 704:768]), block_diagonal(bj[2], bj[3]), NN),
    ]
    update = dot3(bi, split2(jnp.concatenate(half, axis=1)), TN)
    tiles = []
    for p in range(PANEL_T):
        moved = children[p] - update[:, 128 * p : 128 * p + 128]
        tiles.append(got_ref[(meta[128] + p) & 15, 0] + jnp.where(keep[p], moved, 0.0))
    panel = jnp.concatenate(tiles, axis=1)
    panel_ref[...] = panel
    out = dot3(split2(panel), split2(inverse_ref[...]), NN)
    sa_ref[...] = out[0:64]
    sb_ref[...] = out[64:128]


def panel_row(meta, weights, bases, got, inverse):
    return pl.pallas_call(
        panel_kernel,
        grid_spec=pltpu.PrefetchScalarGridSpec(
            num_scalar_prefetch=1, grid=(), in_specs=[whole()] * 4, out_specs=[whole()] * 3
        ),
        out_shape=[
            jax.ShapeDtypeStruct((128, 512), F32),
            jax.ShapeDtypeStruct((64, 512), F32),
            jax.ShapeDtypeStruct((64, 512), F32),
        ],
        compiler_params=pltpu.CompilerParams(vmem_limit_bytes=32 << 20),
        cost_estimate=pl.CostEstimate(flops=4 * 10**8, bytes_accessed=6 << 20, transcendentals=0),
    )(meta, weights, bases, got, inverse)


def moved_kernel(meta, w_ref, base_ref, *refs):
    c_refs, parent_ref, all_ref, g_ref, out_ref = refs[0:4], refs[4], refs[5], refs[6], refs[7]
    col = meta[130]
    bj = []
    for s in range(4):
        j = col_source(meta, s, col)
        bj.append(masked_basis(meta, base_ref, j & 7, 2 * s + (j >> 3), 16 * s + j))
    d01, d03, d22 = (block_diagonal(bj[s], bj[q]) for s, q in ((0, 1), (0, 3), (2, 2)))
    g_ref[0:384] = dot3(split2(w_ref[0, 0:384]), d01, NN)
    g_ref[384:512] = dot3(split2(w_ref[0, 384:512]), d03, NN)
    g_ref[512:640] = dot3(split2(w_ref[0, 512:640]), d22, NN)

    for t in range(8):
        u, w = t // 2, t % 2
        rho = row_source(meta, u)
        bi = split2(masked_basis(meta, base_ref, rho, t, 16 * u + 8 * w + rho))

        def put(s, tile):
            value = c_refs[s][2 * (u - s) + w] - tile
            if u == s:
                keep = rho + 8 * w >= col_source(meta, s, col)
                value = jnp.where(keep, value, 0.0)
            out_ref[u * (u + 1) + w * (u + 1) + s] = value

        def update(first, lane, wide):
            return dot3(bi, split2(g_ref[first : first + 64, lane : lane + wide]), TN)

        if t >= 2:
            both = update(64 * (t - 2), 0, 256)
            put(0, both[:, 0:128])
            put(1, both[:, 128:256])
        else:
            put(0, update(384 + 64 * t, 0, 128))
        if u == 2:
            put(2, update(512 + 64 * w, 0, 128))
        if u == 3:
            put(2, update(512 + 64 * w, 128, 128))
            put(3, update(384 + 64 * w, 128, 128))


    row = meta[129]

    def assemble(a, carry):
        u = a >> 2
        at = 8 * a + row - meta[16 * u]
        for b in range(8):
            s = b // 2
            at_col = 16 * b + col - meta[16 * s]
            use = (at >= 0) & (at < 16) & (at_col >= 0) & (at_col < 16) & (u >= s)
            index = jnp.where(use, u * (u + 1) + (at >> 3) * (u + 1) + s, 0)
            all_ref[a, b] = parent_ref[a, 0, b, 0] + jnp.where(use, out_ref[index], 0.0)
        return carry

    lax.fori_loop(0, 16, assemble, 0)


def assembled_tiles(meta, weights, bases, cols, parent_tiles):
    return pl.pallas_call(
        moved_kernel,
        grid_spec=pltpu.PrefetchScalarGridSpec(
            num_scalar_prefetch=1,
            grid=(),
            in_specs=[whole()] * 7,
            out_specs=whole(),
            scratch_shapes=[pltpu.VMEM((640, 256), F32), pltpu.VMEM((20, 128, 128), F32)],
        ),
        out_shape=jax.ShapeDtypeStruct((16, 8, 128, 128), F32),
        compiler_params=pltpu.CompilerParams(vmem_limit_bytes=24 << 20),
        cost_estimate=pl.CostEstimate(flops=10**9, bytes_accessed=16 << 20, transcendentals=0),
    )(meta, weights, bases, *cols, parent_tiles)


def trailing_kernel(meta, all_ref, *refs):
    a_refs, b_refs, panel_refs, out_ref = refs[0:4], refs[4:8], refs[8:12], refs[12]
    s_ref, p_ref = refs[13:15]
    q, g = pl.program_id(0), pl.program_id(1)
    row, col, start = meta[129], meta[130], meta[128]
    x, z = col >> 2, col & 3

    @pl.when((q == 0) & (g == 0))
    def _():
        for k in range(8):
            tile = gathered_row(meta, k)
            hi, lo = split2(panel_refs[k % 4][k // 4])
            p_ref[tile >> 1, tile & 1] = jnp.concatenate([hi, hi, lo], axis=1)
        for m in range(4):
            for n in range(4):
                hi, lo = split2(a_refs[m][n])
                s_ref[(x - m) & 3, (z - n) & 3, 0:64] = jnp.concatenate([hi, lo, hi], axis=1)
                hi, lo = split2(b_refs[m][n])
                s_ref[(x - n) & 3, (z - m) & 3, 64:128] = jnp.concatenate([hi, lo, hi], axis=1)

    def window(k, j):
        tile_row = 8 * (8 * g + k) + row
        tile_col = 16 * (2 * q + j) + col
        return (tile_row >= tile_col) & (tile_col >= start + PANEL_T)

    first_col = 32 * q + col
    active = (64 * g + 56 + row >= first_col) & (first_col + 16 >= start + PANEL_T)

    @pl.when(active)
    def _():
        right = p_ref[q].reshape(256, 1536)
        for h in range(2):
            left = s_ref[2 * g + h].reshape(512, 1536)
            trailing = lax.dot_general(left, right, (NT, ((), ())), preferred_element_type=F32)
            for k in range(4):
                for j in range(2):
                    part = trailing[128 * k : 128 * k + 128, 128 * j : 128 * j + 128]
                    tile = all_ref[8 * g + 4 * h + k, 2 * q + j]
                    part = jnp.where(window(4 * h + k, j), part, 0.0)
                    out_ref[4 * h + k, 0, j, 0] = tile - part

    @pl.when(jnp.logical_not(active))
    def _():
        for k in range(8):
            for j in range(2):
                out_ref[k, 0, j, 0] = all_ref[8 * g + k, 2 * q + j]


def trailing_update(meta, assembled, shape, sa, sb, panel):
    tiles = pl.BlockSpec((8, 1, 2, 1, 128, 128), lambda q, g, meta: (g, 0, q, 0, 0, 0))
    return pl.pallas_call(
        trailing_kernel,
        grid_spec=pltpu.PrefetchScalarGridSpec(
            num_scalar_prefetch=1,
            grid=(4, 2),
            in_specs=[whole()] * 13,
            out_specs=tiles,
            scratch_shapes=[
                pltpu.VMEM((4, 4, 128, 1536), BF16),
                pltpu.VMEM((4, 2, 128, 1536), BF16),
            ],
        ),
        out_shape=jax.ShapeDtypeStruct(shape, F32),
        compiler_params=pltpu.CompilerParams(vmem_limit_bytes=24 << 20),
        cost_estimate=pl.CostEstimate(flops=7 * 10**9, bytes_accessed=24 << 20, transcendentals=0),
    )(meta, assembled, *sa, *sb, *panel)


def per_device(
    contribution,
    parent_tiles,
    row_basis,
    pivot_basis,
    tile_ranks,
    block_map,
    panel_start,
    pivot_inverse,
):
    my_row = lax.axis_index("row")
    my_col = lax.axis_index("col")
    meta = jnp.concatenate(
        [block_map, tile_ranks, panel_start, jnp.stack([my_row, my_col])]
    ).astype(jnp.int32)
    shifts = [block_map[16 * u] - 32 * u for u in range(4)]

    last = rotate(contribution[6:, 0, 3, 0], "col", 16, shifts[3])
    tiles = [contribution[2 * u : 2 * u + 2, 0, 0 : u + 1, 0] for u in range(3)]
    tiles.append(jnp.concatenate([contribution[6:, 0, 0:3, 0], last[:, None]], axis=1))
    pivots = gather_rows(pivot_basis[:, 0], *tiles)
    parts = products(meta, pivots)
    weights = lax.psum_scatter(parts, "col", scatter_dimension=0, tiled=True)
    rows = [rotate(after(tiles[u], parts), "row", 8, shifts[u] & 7) for u in range(4)]
    picked = panel_pick(meta, parent_tiles, rows)
    got = across_col(picked)
    bases = lax.all_gather(after(row_basis[:, 0], picked), "row", axis=0)
    cols = [
        rotate(
            after(jnp.concatenate([rows[u][:, s] for u in range(s, 4)]), picked),
            "col",
            16,
            shifts[s],
        )
        for s in range(3)
    ]
    cols.append(rows[3][:, 3])
    panel, sa, sb = panel_row(meta, after(weights, *cols), bases, got, pivot_inverse)
    turn = []
    for r in range(8):
        for c in range(16):
            turn.append((16 * r + c, 16 * (c // 2) + 8 * (c % 2) + r))
    panel = lax.ppermute(panel, ("row", "col"), turn)
    ring_a = jnp.stack([sa] + [col_perm(sa, 0, d) for d in (1, 2, 3)])
    ring_b = jnp.stack([sb] + [col_perm(sb, d, 0) for d in (1, 2, 3)])
    swapped = row_perm(panel, 0, 1)
    late_a, late_b = after(ring_a, swapped), after(ring_b, swapped)
    sa = [ring_a] + [col_perm(late_a if d == 2 else ring_a, d, 0) for d in (1, 2, 3)]
    sb = [ring_b] + [col_perm(late_b if d == 2 else ring_b, 0, d) for d in (1, 2, 3)]
    panel = jnp.stack([panel, swapped])
    panel = [panel] + [row_perm(panel, d, 0) for d in (1, 2, 3)]
    assembled = assembled_tiles(meta, weights, bases, cols, parent_tiles)
    return trailing_update(meta, assembled, parent_tiles.shape, sa, sb, panel)


def solution(mesh):
    placed = (
        P(None, "row", None, "col", None, None),
        P(None, "row", None, "col", None, None),
        P(None, "row", None, None),
        P(None, "row", None, "col"),
        P(),
        P(),
        P(),
        P(),
    )
    return jax.shard_map(
        per_device,
        mesh=mesh,
        in_specs=placed,
        out_specs=P(None, "row", None, "col", None, None),
        check_vma=False,
    )
```
